32 devices in a mesh: tm: 8 (over z, x), lat: 4 (over y, core).
Axes of the slice: x: 2, y: 2, z: 4, core: 2. Of those that a mesh axis runs over, the one named last changes fastest.
Arguments:
- states: float32 [8, 3, 32, 2048], P('tm', None, 'lat'), may hold values from -1.5 to 1.5
- background: float32 [3, 32, 2048], P(None, 'lat'), may hold values from -1.5 to 1.5
- error_std: float32 [3, 32, 2048], P(None, 'lat'), may hold values from 0.5 to 2
- land_mask: int32 [8, 128], P('lat'), may hold values 0 or 1
- obs_cells: int32 [8, 512], P('tm', 'lat'), may hold values from 0 to 16383
- measurement_moments: int32 [8, 512], P('tm', 'lat'), may hold values from 0 to 3
- obs_values: float32 [8, 512], P('tm', 'lat'), may hold values from -2.4 to 2.4
- obs_error: float32 [8, 512], P('tm', 'lat'), may hold values from 0.3 to 1
Outputs:
- estimated_openings: float32 [8, 3, 32, 2048], P('tm', None, 'lat')
- slid: float32 [8, 3, 32, 2048], P('tm', None, 'lat')
- costs: float32 [2], replicated
The draws below stay inside these ranges and needn't reach their ends.
Inputs may be any that keep to these rules, and one draw needn't show every extreme that they name: `obs_cells`: cell index within the band: row within the band times 2048 plus column. `land_mask`: each entry covers 4 x 16 cells.
All inputs are finite; a program needn't handle non-finite values. No bound on the sum of `land_mask` on one device may be relied on, other than what follows from the above.
Results may differ from the reference program's by a relative error of at most 0.0003.
Values sent between devices are 32-bit elements; how exact they have to be, the bound alone decides.
A program may use at most 64 MiB of HBM per device.

```python
import math
import jax
import jax.numpy as jnp
from jax import lax

LAT_DEV = 8
NLON = 2048
OBS_DEV = 128
STEPS = 4
ITERS = 2
TILE_LAT = 4
TILE_LON = 16
NT = 8
NLAT = 32
OBS = 512
N_TM = 8
N_LAT = 4


def draw_obs_values(key, part):
    window_rows = jnp.arange(NT, dtype=jnp.float32)[:, None]
    rising = 1.0 + 2.0 * window_rows / max(NT - 1, 1)
    base_values = jnp.clip(jax.random.normal(key, (NT, OBS), jnp.float32), -4.0, 4.0) * 0.2
    return jnp.clip(base_values * rising, -2.4, 2.4)


def touch_ends(array, key, low, high):
    extent = array.shape
    spot = [jax.random.randint(jax.random.fold_in(key, axis), (), 0, extent[axis]) for axis in range(len(extent))]
    array = array.at[tuple(spot)].set(low)
    longest = extent.index(max(extent))
    spot[longest] = (spot[longest] + 1) % extent[longest]
    return array.at[tuple(spot)].set(high)


def level_of(key, dims, split, least, largest):
    level = 1.0
    for position, shards_of in split:
        heights = jax.random.uniform(jax.random.fold_in(jax.random.fold_in(key, 6), position), (shards_of,), jnp.float32, least / len(split), largest / len(split))
        level = level * jnp.repeat(jnp.exp(heights), dims[position] // shards_of).reshape((-1,) + (1,) * (len(dims) - 1 - position))
    return level


def noise(stream_key, extent, scale, reach, shards=(), kind=jnp.bfloat16):
    array = jax.random.normal(stream_key, extent, jnp.float32) * scale
    if len(shards) > 0:
        array = level_of(stream_key, extent, shards, -0.22, 0.18) * array
    return jnp.clip(array, min=-reach, max=reach).astype(kind)


def setup_inputs(seed: int = 0) -> dict:
    splits = jax.random.split(jax.random.key(seed), 9)
    return {
        "states": noise(splits[0], (NT, 3, NLAT, NLON), 0.3, 1.5, ((0, 8), (2, 4)), jnp.float32),
        "background": noise(splits[1], (3, NLAT, NLON), 0.3, 1.5, ((1, 4),), jnp.float32),
        "error_std": jnp.clip(jnp.exp(math.log(2.0) - 1.3862944 * jax.random.uniform(splits[2], (3, NLAT, NLON), jnp.float32) ** level_of(splits[2], (3, NLAT, NLON), ((1, 4),), -0.2, 0.2)), 0.5, 2.0),
        "land_mask": touch_ends((jax.random.randint(splits[3], (NLAT // TILE_LAT, NLON // TILE_LON), 0, 8) < 7).astype(jnp.int32), jax.random.fold_in(splits[3], 1), 0, 1),
        "obs_cells": touch_ends(jax.random.randint(splits[4], (NT, OBS), 0, LAT_DEV * NLON), jax.random.fold_in(splits[4], 1), 0, (LAT_DEV * NLON) - 1).astype(jnp.int32),
        "measurement_moments": touch_ends(jax.random.randint(splits[5], (NT, OBS), 0, STEPS), jax.random.fold_in(splits[5], 1), 0, STEPS - 1).astype(jnp.int32),
        "obs_values": draw_obs_values(jax.random.fold_in(splits[8], 71), 0),
        "obs_error": jnp.clip(jnp.exp(math.log(1.0) - 1.2039728 * jax.random.uniform(splits[7], (NT, OBS), jnp.float32) ** level_of(splits[7], (NT, OBS), ((0, 8), (1, 4)), -0.2, 0.2)), 0.3, 1.0),
    }


TIME_STEP = 0.25
MEAN_DEPTH = 1.0
GRAVITY = 1.0
DRAG_RATE = 0.02
STEP_LENGTH = 0.3
CORIOLIS_MEAN = 0.3
CORIOLIS_SLOPE = 0.2
EPSILON = 1e-06

def expand_mask(land_mask):
    tiles_lat, tiles_lon = land_mask.shape
    grown = jnp.broadcast_to(land_mask[:, None, :, None], (tiles_lat, TILE_LAT, tiles_lon, TILE_LON))
    return grown.reshape(tiles_lat * TILE_LAT, tiles_lon * TILE_LON).astype(jnp.float32)

def zonal_diff(field):
    return 0.5 * (jnp.roll(field, -1, axis=1) - jnp.roll(field, 1, axis=1))

def merid_diff(field):
    return 0.5 * (field[2:] - field[:-2])

def model_step(padded, coriolis, ocean_mask):
    interior = padded[:, 1:-1]
    height, eastward, northward = (interior[0], interior[1], interior[2])
    height_pad, east_pad, north_pad = (padded[0], padded[1], padded[2])
    d_height = -(zonal_diff((MEAN_DEPTH + height) * eastward) + merid_diff((MEAN_DEPTH + height_pad) * north_pad))
    d_east = coriolis * northward - GRAVITY * zonal_diff(height) - eastward * zonal_diff(eastward) - northward * merid_diff(east_pad) - DRAG_RATE * eastward
    d_north = -coriolis * eastward - GRAVITY * merid_diff(height_pad) - eastward * zonal_diff(northward) - northward * merid_diff(north_pad) - DRAG_RATE * northward
    return interior + TIME_STEP * ocean_mask * jnp.stack([d_height, d_east, d_north])

def reference(states, background, error_std, land_mask, obs_cells, measurement_moments, obs_values, obs_error):
    ocean_mask = expand_mask(land_mask)
    total_rows = LAT_DEV * N_LAT
    latitude = jnp.arange(total_rows, dtype=jnp.float32)[:, None]
    coriolis = CORIOLIS_MEAN + CORIOLIS_SLOPE * (latitude / total_rows - 0.5)
    band_index = jnp.arange(OBS_DEV * N_LAT, dtype=jnp.int32) // OBS_DEV
    linear_grid_points = (obs_cells + (band_index * (LAT_DEV * NLON))[None, :]).astype(jnp.int32)
    variance = error_std * error_std
    precision = 1.0 / (obs_error * obs_error)
    cell_count = 3 * total_rows * NLON

    def run(current, cell_ids, obs_times):
        measured_quantities = jnp.zeros(cell_ids.shape, jnp.float32)
        for substep in range(STEPS):
            padded = jnp.pad(current, ((0, 0), (1, 1), (0, 0)))
            values = jnp.take(current[0].reshape(-1), cell_ids)
            measured_quantities = measured_quantities + jnp.where(obs_times == substep, values, 0.0)
            current = model_step(padded, coriolis, ocean_mask)
        return (current, measured_quantities)

    def integrate_segment_parts(members):
        return run(members[0], members[1], members[2])

    def pullback(members):
        current, cell_ids, obs_times, force, obs_force = members
        _, backward = jax.vjp(lambda start: run(start, cell_ids, obs_times), current)
        return backward((force, obs_force))[0]
    estimated_openings = states
    costs = []
    for iteration in range(ITERS):
        predicted_closing_condition, measured_quantities = lax.map(integrate_segment_parts, (estimated_openings, linear_grid_points, measurement_moments))
        prior_interval = jnp.concatenate([jnp.zeros_like(predicted_closing_condition[:1]), predicted_closing_condition[:-1]])
        own_term = jnp.concatenate([(estimated_openings[:1] - background[None]) / variance[None], (estimated_openings[1:] - prior_interval[1:]) / variance[None]])
        end_force = -jnp.concatenate([own_term[1:], jnp.zeros_like(own_term[:1])])
        misfit = measured_quantities - obs_values
        weighted = misfit * precision
        total_cost = 0.5 * (jnp.sum(misfit * weighted) + jnp.sum(own_term * own_term * variance[None]))
        adjoint_start = lax.map(pullback, (estimated_openings, linear_grid_points, measurement_moments, end_force, weighted))
        gradient = own_term + adjoint_start
        direction = variance[None] * gradient
        steepness = jnp.sum(gradient * direction)
        step_scale = STEP_LENGTH / jnp.sqrt(steepness / (N_TM * cell_count) + EPSILON)
        estimated_openings = estimated_openings - step_scale * direction
        costs.append(total_cost / cell_count)
    final_end, _ = lax.map(integrate_segment_parts, (estimated_openings, linear_grid_points, measurement_moments))
    slid = jnp.concatenate([estimated_openings[1:], final_end[-1:]])
    return (estimated_openings, slid, jnp.stack(costs))
```

```python
import functools

import jax
import jax.numpy as jnp
from jax import lax
from jax.experimental import pallas as pl
from jax.experimental.pallas import tpu as pltpu
from jax.sharding import PartitionSpec as P

STEPS = 4
ITERS = 2
TILE_LAT = 4
TILE_LON = 16

TIME_STEP = 0.25
MEAN_DEPTH = 1.0
DRAG_RATE = 0.02
STEP_LENGTH = 0.3
CORIOLIS_MEAN = 0.3
CORIOLIS_SLOPE = 0.2
EPSILON = 1e-06

MESH = pl.DeviceIdType.MESH
LANES = 128
DIRECT_MAX = 64
KERNEL_VMEM = 24 * 2**20
WRITE_VMEM = 2**20


def split3(x):
    hi = x.astype(jnp.bfloat16)
    rest = x - hi.astype(jnp.float32)
    mid = rest.astype(jnp.bfloat16)
    low = (rest - mid.astype(jnp.float32)).astype(jnp.bfloat16)
    return jnp.concatenate([hi, mid, low], axis=0)


def join3(y):
    n = y.shape[0] // 3
    return (y[2 * n :] + y[n : 2 * n]) + y[:n]


def fold_lanes(x):
    total = x[:, :LANES]
    for c in range(LANES, x.shape[1], LANES):
        total = total + x[:, c : c + LANES]
    return jnp.sum(total, axis=0, keepdims=True)


def kernel(
    n_tm, n_lat,
    states_hbm, background_hbm, error_hbm, mask_hbm, cells_hbm, moments_hbm, values_hbm, obs_err_hbm,
    est_out, slid_out, costs_out,
    xs, deriv, lam, onehot, gain, cor, masks, variance, inv_var,
    xnext, fe_prev, adj_in, dir_buf, dir_halo, dir_next, parts, parts_tm,
    error_std, land_mask, obs_cells, obs_moments, obs_values, obs_error,
    ssem, rsem, lsem, known,
):
    tm = lax.axis_index("tm")
    lat = lax.axis_index("lat")
    rows = variance.shape[1]
    lon = variance.shape[2]
    wide = 2 * rows
    half = STEPS
    total_rows = rows * n_lat
    cell_count = 3 * total_rows * lon
    n_dev = n_tm * n_lat
    me = tm * n_lat + lat
    has_up = lat > 0
    has_down = lat < n_lat - 1
    has_prev = tm > 0
    has_next = tm < n_tm - 1
    up = {"lat": lat - 1}
    down = {"lat": lat + 1}
    before = {"tm": tm - 1}
    after = {"tm": tm + 1}
    direct = n_dev <= DIRECT_MAX

    def wrapped(i, n):
        return jnp.where(i >= n, i - n, i)

    lats = [lat] + [wrapped(lat + d, n_lat) for d in range(1, n_lat)]
    tms = [tm] + [wrapped(tm + d, n_tm) for d in range(1, n_tm)]
    lat_partners = [{"lat": lats[d]} for d in range(1, n_lat)]
    tm_partners = [{"tm": tms[d]} for d in range(1, n_tm)]
    if direct:
        pairs = [(t, d) for t in range(n_tm) for d in range(n_lat) if t or d]
        if n_tm & (n_tm - 1) == 0 and n_lat & (n_lat - 1) == 0:
            pairs.sort(key=lambda p: -(p[0] // 2 + p[0] % 2 + p[1] // 2 + 0.1 * (p[1] % 2)))
            all_partners = [
                {"tm": jnp.bitwise_xor(tm, t), "lat": jnp.bitwise_xor(lat, d)} for t, d in pairs
            ]
        else:
            all_partners = [{"tm": tms[t], "lat": lats[d]} for t, d in pairs]
    barrier = pltpu.get_barrier_semaphore()
    greeted = [(None, p) for p in lat_partners] + [(has_prev, before), (has_next, after)]

    def guarded(cond, action):
        if cond is None:
            action()
        else:
            pl.when(cond)(action)

    for cond, partner in greeted:
        guarded(cond, lambda partner=partner: pl.semaphore_signal(
            barrier, inc=1, device_id=partner, device_id_type=MESH))
    reaches = []
    while 2 ** len(reaches) < n_tm:
        reaches.append(2 ** len(reaches))

    def tell(stage):
        d = reaches[stage]
        for cond, target in ((tm >= d, tm - d), (tm + d < n_tm, tm + d)):
            @pl.when(cond)
            def _(target=target):
                pl.semaphore_signal(
                    known.at[stage], inc=1, device_id={"tm": target}, device_id_type=MESH
                )

    def hear(stage):
        d = reaches[stage]
        pl.semaphore_wait(
            known.at[stage], (tm >= d).astype(jnp.int32) + (tm + d < n_tm).astype(jnp.int32)
        )

    own = slice(0, rows)
    loads = []

    def load(src, dst):
        copy = pltpu.make_async_copy(src, dst, lsem.at[len(loads)])
        copy.start()
        loads.append(copy)

    load(states_hbm.at[0], xs.at[0, :, own])
    load(mask_hbm, land_mask)
    load(error_hbm, error_std)
    load(cells_hbm, obs_cells)
    load(moments_hbm, obs_moments)
    load(values_hbm, obs_values)
    load(obs_err_hbm, obs_error)
    for it in range(ITERS):
        @pl.when(tm == 0)
        def _(it=it):
            pltpu.make_async_copy(background_hbm, fe_prev.at[it], lsem.at[7 + it]).start()

    def remote(src, dst, k, device):
        return pltpu.make_async_remote_copy(
            src_ref=src, dst_ref=dst, send_sem=ssem.at[k], recv_sem=rsem.at[k],
            device_id=device, device_id_type=MESH,
        )

    pending = []
    late = []

    def send(cond, src, dst, k, device, queue=pending):
        @pl.when(cond)
        def _():
            remote(src, dst, k, device).start()

        queue.append((cond, src, k, device))

    def drain(queue):
        for cond, src, k, device in queue:
            @pl.when(cond)
            def _(src=src, k=k, device=device):
                remote(src, src, k, device).wait_send()
        queue.clear()

    def arrive(cond, dst, k, device):
        @pl.when(cond)
        def _():
            remote(dst, dst, k, device).wait_recv()

    zeros_half = jnp.zeros((3, half, lon), jnp.float32)
    lo, hi = slice(0, half), slice(half, rows)
    lo_w, hi_w = slice(rows, rows + half), slice(rows + half, wide)

    @pl.when(lat == n_lat - 1)
    def _():
        xs[0, :, lo_w, :] = zeros_half
        masks[lo_w, :] = jnp.zeros((half, LANES), jnp.float32)
        for it in range(ITERS):
            adj_in[it, :, hi, :] = zeros_half
            dir_halo[it, :, lo, :] = zeros_half

    @pl.when(lat == 0)
    def _():
        xs[0, :, hi_w, :] = zeros_half
        masks[hi_w, :] = jnp.zeros((half, LANES), jnp.float32)
        for it in range(ITERS):
            adj_in[it, :, lo, :] = zeros_half
            dir_halo[it, :, hi, :] = zeros_half

    @pl.when(tm == n_tm - 1)
    def _():
        xnext[...] = jnp.zeros(xnext.shape, jnp.float32)
        for it in range(ITERS):
            dir_next[it] = jnp.zeros(xnext.shape, jnp.float32)

    loads[1].wait()
    mask = land_mask[...].astype(jnp.float32)
    tile_cols = mask.shape[1]
    masks[own, :] = jnp.concatenate(
        [jnp.broadcast_to(mask[i : i + 1], (TILE_LAT, tile_cols)) for i in range(rows // TILE_LAT)],
        axis=0,
    )

    loads[0].wait()
    pl.semaphore_wait(
        barrier, len(lat_partners) + has_prev.astype(jnp.int32) + has_next.astype(jnp.int32)
    )

    send(has_up, masks.at[lo], masks.at[lo_w], 0, up)
    send(has_down, masks.at[hi], masks.at[hi_w], 1, down)
    send(has_up, xs.at[0, :, lo], xs.at[0, :, lo_w], 2, up)
    send(has_down, xs.at[0, :, hi], xs.at[0, :, hi_w], 3, down)
    send(has_prev, xs.at[0, :, own], xnext, 4, before)
    if reaches:
        tell(0)

    for copy in loads[2:]:
        copy.wait()
    var = error_std[...] * error_std[...]
    variance[...] = var
    inv_var[...] = 1.0 / var
    cells = obs_cells[...]
    n_obs = cells.shape[1]
    cell_row = jnp.zeros_like(cells)
    for r in range(1, rows):
        cell_row = cell_row + (cells >= r * lon).astype(jnp.int32)
    cell_col = cells - cell_row * lon
    onehot[...] = (
        lax.broadcasted_iota(jnp.int32, (lon, n_obs), 0) == cell_col
    ).astype(jnp.float32).astype(jnp.bfloat16)
    taken = (
        lax.broadcasted_iota(jnp.int32, (STEPS * rows, n_obs), 0)
        == obs_moments[...] * rows + cell_row
    ).astype(jnp.float32)
    targets = obs_values[...]
    precision = 1.0 / (obs_error[...] * obs_error[...])
    r_id = lax.broadcasted_iota(jnp.int32, (wide, LANES), 0)
    r_id = jnp.where(r_id < rows + half, r_id, r_id - wide) + lat * rows
    cor[...] = 2.0 * (CORIOLIS_MEAN + CORIOLIS_SLOPE * (r_id.astype(jnp.float32) / total_rows - 0.5))

    arrive(has_down, masks.at[lo_w], 0, down)
    arrive(has_up, masks.at[hi_w], 1, up)
    first_col = lax.broadcasted_iota(jnp.int32, (tile_cols, lon), 0) * TILE_LON
    col = lax.broadcasted_iota(jnp.int32, (tile_cols, lon), 1)
    grow = ((col >= first_col) & (col < first_col + TILE_LON)).astype(jnp.float32)
    gain[...] = (0.5 * TIME_STEP) * jnp.dot(
        masks[...].astype(jnp.bfloat16), grow.astype(jnp.bfloat16),
        preferred_element_type=jnp.float32,
    )
    arrive(has_down, xs.at[0, :, lo_w], 2, down)
    arrive(has_up, xs.at[0, :, hi_w], 3, up)
    if len(reaches) > 1:
        hear(0)
        tell(1)

    def east(a):
        return pltpu.roll(a, lon - 1, 1)

    def west(a):
        return pltpu.roll(a, 1, 1)

    def north(a):
        return pltpu.roll(a, wide - 1, 0)

    def south(a):
        return pltpu.roll(a, 1, 0)

    def dx2(a):
        return east(a) - west(a)

    def dy2(a):
        return north(a) - south(a)

    def coriolis2(n):
        return jnp.concatenate([cor[0:n]] * (lon // LANES), axis=-1)

    def forward_step(s, n):
        h, u, v = xs[s, 0] + MEAN_DEPTH, xs[s, 1], xs[s, 2]
        h_n, h_s, u_n, u_s = north(h)[:n], south(h)[:n], north(u)[:n], south(u)[:n]
        v_n, v_s = north(v)[:n], south(v)[:n]
        h, u, v = h[:n], u[:n], v[:n]
        h_e, h_w, u_e, u_w, v_e, v_w = east(h), west(h), east(u), west(u), east(v), west(v)
        g = gain[0:n]
        f2 = coriolis2(n)
        drag_u = (u_e - u_w) + 2.0 * DRAG_RATE
        turn_u = f2 - (u_n - u_s)
        turn_v = f2 + (v_e - v_w)
        drag_v = (v_n - v_s) + 2.0 * DRAG_RATE
        xs[s + 1, 0, 0:n] = xs[s, 0, 0:n] - g * ((h_e * u_e - h_w * u_w) + (h_n * v_n - h_s * v_s))
        xs[s + 1, 1, 0:n] = u + g * (v * turn_u - u * drag_u - (h_e - h_w))
        xs[s + 1, 2, 0:n] = v - g * (u * turn_v + v * drag_v + (h_n - h_s))
        return drag_u, turn_u, turn_v, drag_v

    def forward(keep):
        for s in range(STEPS):
            n = rows if s == STEPS - 1 else wide
            terms = forward_step(s, n)
            if keep:
                for i, term in enumerate(terms):
                    deriv[s, i, 0:n] = term

    def padded(a):
        return jnp.concatenate([a, jnp.zeros((rows, lon), jnp.float32)], axis=0)

    def adjoint_last(closing, forcing):
        s = STEPS - 1
        g = gain[own]
        a, b, c = closing[0] * g, closing[1] * g, closing[2] * g
        h, u, v = xs[s, 0] + MEAN_DEPTH, xs[s, 1, own], xs[s, 2]
        b_all, c_all = padded(b), padded(c)
        ax, ay, cy = dx2(a), dy2(padded(a)), dy2(c_all)
        vb, vc = dy2(v * b_all), dy2(v * c_all)
        v_ay, h_ay = v * ay, h * ay
        lam[s, 0, own] = closing[0] + forcing + u * ax + v_ay[:rows] + dx2(b) + cy[:rows]
        lam[s, 0, rows:wide] = v_ay[rows:] + cy[rows:]
        lam[s, 1, own] = (
            closing[1] + h[:rows] * ax + dx2(u * b) + vb[:rows]
            - b * deriv[s, 0, own] - c * deriv[s, 2, own]
        )
        lam[s, 1, rows:wide] = vb[rows:]
        lam[s, 2, own] = (
            closing[2] + h_ay[:rows] + dx2(u * c) + vc[:rows]
            + b * deriv[s, 1, own] - c * deriv[s, 3, own]
        )
        lam[s, 2, rows:wide] = h_ay[rows:] + vc[rows:]

    def adjoint_step(s, forcing):
        g = gain[...]
        lh, lu, lv = lam[s + 1, 0], lam[s + 1, 1], lam[s + 1, 2]
        a, b, c = lh * g, lu * g, lv * g
        h, u, v = xs[s, 0] + MEAN_DEPTH, xs[s, 1], xs[s, 2]
        ax, ay = dx2(a), dy2(a)
        b_e, b_w, u_e, u_w = east(b), west(b), east(u), west(u)
        c_n, c_s, v_n, v_s = north(c), south(c), north(v), south(v)
        new_h = lh + u * ax + v * ay + (b_e - b_w) + (c_n - c_s)
        lam[s, 0, own] = new_h[:rows] + forcing
        lam[s, 0, rows:wide] = new_h[rows:]
        lam[s, 1] = (
            lu + h * ax + (u_e * b_e - u_w * b_w) + dy2(v * b)
            - b * deriv[s, 0] - c * deriv[s, 2]
        )
        lam[s, 2] = (
            lv + h * ay + dx2(u * c) + (v_n * c_n - v_s * c_s)
            + b * deriv[s, 1] - c * deriv[s, 3]
        )

    def exchange(buf, value, k, size, mine, partner):
        buf[mine] = value
        for device in partner:
            remote(buf.at[mine], buf.at[mine], k, device).start()

    def collect(buf, k, size, partner):
        remote(buf.at[0 : size - 1], buf.at[0 : size - 1], k, partner[0]).wait_recv()
        total = jnp.sum(buf[...], axis=0)
        return total

    def sent(buf, k, size, partner):
        remote(buf.at[0 : size - 1], buf.at[0 : size - 1], k, partner[0]).wait_send()

    scale = None
    for it in range(ITERS):
        base = 5 + 8 * it
        forward(True)
        send(has_next, xs.at[STEPS, :, own], fe_prev.at[it], base, after)

        heights = jnp.concatenate([xs[s, 0, own, :] for s in range(STEPS)], axis=0)
        seen = join3(
            jnp.dot(split3(heights), onehot[...], preferred_element_type=jnp.float32)
        )
        misfit = jnp.sum(seen * taken, axis=0, keepdims=True) - targets
        weighted = misfit * precision
        spread = join3(
            lax.dot_general(
                split3(taken * weighted), onehot[...], (((1,), (1,)), ((), ())),
                preferred_element_type=jnp.float32,
            )
        )
        if it == 0:
            arrive(has_next, xnext, 4, after)
        else:
            arrive(has_next, dir_next.at[it - 1], base - 8 + 5, after)
            xnext[...] = xnext[...] - scale * dir_next[it - 1]

        if it == 0:
            for stage in range(1, len(reaches)):
                hear(stage)
                if stage + 1 < len(reaches):
                    tell(stage + 1)
            if len(reaches) == 1:
                hear(0)
        closing = jnp.where(has_next, (xs[STEPS, :, own, :] - xnext[...]) * inv_var[...], 0.0)
        adjoint_last(closing, spread[(STEPS - 1) * rows : STEPS * rows])
        for s in reversed(range(STEPS - 1)):
            adjoint_step(s, spread[s * rows : (s + 1) * rows])
        send(has_down, lam.at[0, :, lo_w], adj_in.at[it, :, lo], base + 1, down)
        send(has_up, lam.at[0, :, hi_w], adj_in.at[it, :, hi], base + 2, up)

        arrive(has_prev, fe_prev.at[it], base, before)

        @pl.when(tm == 0)
        def _():
            pltpu.make_async_copy(background_hbm, fe_prev.at[it], lsem.at[7 + it]).wait()

        cost = misfit * weighted
        for f in range(3):
            gap = xs[0, f, own, :] - fe_prev[it, f]
            cost = cost + fold_lanes(gap * gap * inv_var[f])
            dir_buf[it, f] = gap + variance[f] * lam[0, f, own, :]
        arrive(has_up, adj_in.at[it, :, lo], base + 1, up)
        arrive(has_down, adj_in.at[it, :, hi], base + 2, down)
        steep = jnp.zeros((1, LANES), jnp.float32)
        for f in range(3):
            direction = dir_buf[it, f] + variance[f] * adj_in[it, f]
            dir_buf[it, f] = direction
            steep = steep + fold_lanes(direction * direction * inv_var[f])

        message = jnp.concatenate([steep, cost], axis=0)
        if direct:
            exchange(parts.at[it], message, base + 6, n_dev, me, all_partners)
        else:
            exchange(parts.at[it], message, base + 6, n_lat, lat, lat_partners)
        send(has_up, dir_buf.at[it, :, lo], dir_halo.at[it, :, lo], base + 3, up, late)
        send(has_down, dir_buf.at[it, :, hi], dir_halo.at[it, :, hi], base + 4, down, late)
        drain(pending)
        if direct:
            send(has_prev, dir_buf.at[it], dir_next.at[it], base + 5, before, late)
            total = collect(parts.at[it], base + 6, n_dev, all_partners)
        else:
            total = collect(parts.at[it], base + 6, n_lat, lat_partners)
            exchange(parts_tm.at[it], total, base + 7, n_tm, tm, tm_partners)
            send(has_prev, dir_buf.at[it], dir_next.at[it], base + 5, before, late)
            total = collect(parts_tm.at[it], base + 7, n_tm, tm_partners)
        steepness = jnp.sum(total[0:1], axis=1, keepdims=True)
        scale = STEP_LENGTH / jnp.sqrt(steepness / (n_tm * cell_count) + EPSILON)
        costs_out[it : it + 1] = jnp.broadcast_to(
            jnp.sum(total[1:2], axis=1, keepdims=True) * (0.5 / cell_count), (1, LANES)
        )

        for f in range(3):
            moved = xs[0, f, own, :] - scale * dir_buf[it, f]
            xs[0, f, own, :] = moved
            if it == ITERS - 1:
                est_out[0, f] = moved
        arrive(has_down, dir_halo.at[it, :, lo], base + 3, down)
        arrive(has_up, dir_halo.at[it, :, hi], base + 4, up)
        for f in range(3):
            xs[0, f, rows:wide, :] = xs[0, f, rows:wide, :] - scale * dir_halo[it, f]

    @pl.when(tm == n_tm - 1)
    def _():
        forward(False)
        slid_out[0] = xs[STEPS, :, own, :]

    arrive(has_next, dir_next.at[ITERS - 1], 5 + 8 * (ITERS - 1) + 5, after)

    @pl.when(has_next)
    def _():
        slid_out[0] = xnext[...] - scale * dir_next[ITERS - 1]

    drain(late)
    for it in range(ITERS):
        base = 5 + 8 * it
        if direct:
            sent(parts.at[it], base + 6, n_dev, all_partners)
        else:
            sent(parts.at[it], base + 6, n_lat, lat_partners)
            sent(parts_tm.at[it], base + 7, n_tm, tm_partners)


def write_out(est, slid, costs, est_out, slid_out, costs_out, held, sem):
    moves = [
        pltpu.make_async_copy(est, est_out, sem.at[0]),
        pltpu.make_async_copy(slid, slid_out, sem.at[1]),
        pltpu.make_async_copy(held, costs_out, sem.at[2]),
    ]
    moves[0].start()
    moves[1].start()
    for it in range(ITERS):
        held[it] = costs[it, 0]
    moves[2].start()
    for copy in moves:
        copy.wait()


def shards(n_tm, n_lat, *args):
    states, background = args[0], args[1]
    _, rows, lon = background.shape
    n_obs = args[4].shape[1]
    wide = 2 * rows
    f32 = jnp.float32
    direct = n_tm * n_lat <= DIRECT_MAX
    field = (3, rows, lon)
    sems = 5 + 8 * ITERS
    est, slid, costs = pl.pallas_call(
        functools.partial(kernel, n_tm, n_lat),
        out_shape=(
            pltpu.VMEM(states.shape, f32),
            pltpu.VMEM(states.shape, f32),
            pltpu.VMEM((ITERS, LANES), f32),
        ),
        in_specs=[pl.BlockSpec(memory_space=pltpu.HBM)] * 8,
        out_specs=(pl.BlockSpec(memory_space=pltpu.VMEM),) * 3,
        scratch_shapes=[
            pltpu.VMEM((STEPS + 1, 3, wide, lon), f32),
            pltpu.VMEM((STEPS, 4, wide, lon), f32),
            pltpu.VMEM((STEPS, 3, wide, lon), f32),
            pltpu.VMEM((lon, n_obs), jnp.bfloat16),
            pltpu.VMEM((wide, lon), f32),
            pltpu.VMEM((wide, LANES), f32),
            pltpu.VMEM((wide, LANES), f32),
            pltpu.VMEM(field, f32),
            pltpu.VMEM(field, f32),
            pltpu.VMEM(field, f32),
            pltpu.VMEM((ITERS,) + field, f32),
            pltpu.VMEM((ITERS,) + field, f32),
            pltpu.VMEM((ITERS,) + field, f32),
            pltpu.VMEM((ITERS,) + field, f32),
            pltpu.VMEM((ITERS,) + field, f32),
            pltpu.VMEM((ITERS, n_tm * n_lat if direct else n_lat, 2, LANES), f32),
            pltpu.VMEM((ITERS, n_tm, 2, LANES), f32),
            pltpu.VMEM(field, f32),
            pltpu.VMEM(args[3].shape, jnp.int32),
            pltpu.VMEM((1, n_obs), jnp.int32),
            pltpu.VMEM((1, n_obs), jnp.int32),
            pltpu.VMEM((1, n_obs), f32),
            pltpu.VMEM((1, n_obs), f32),
            pltpu.SemaphoreType.DMA((sems,)),
            pltpu.SemaphoreType.DMA((sems,)),
            pltpu.SemaphoreType.DMA((7 + ITERS,)),
            pltpu.SemaphoreType.REGULAR((max(n_tm.bit_length(), 1),)),
        ],
        compiler_params=pltpu.CompilerParams(
            collective_id=0, has_side_effects=True, vmem_limit_bytes=KERNEL_VMEM
        ),
    )(*[pltpu.with_memory_space_constraint(a, pltpu.HBM) for a in args])
    return pl.pallas_call(
        write_out,
        out_shape=(
            jax.ShapeDtypeStruct(states.shape, f32),
            jax.ShapeDtypeStruct(states.shape, f32),
            jax.ShapeDtypeStruct((ITERS,), f32),
        ),
        in_specs=[pl.BlockSpec(memory_space=pltpu.VMEM)] * 3,
        out_specs=(pl.BlockSpec(memory_space=pltpu.HBM),) * 3,
        scratch_shapes=[pltpu.SMEM((ITERS,), f32), pltpu.SemaphoreType.DMA((3,))],
        compiler_params=pltpu.CompilerParams(vmem_limit_bytes=WRITE_VMEM),
    )(est, slid, costs)


def solution(mesh):
    placed = (
        P("tm", None, "lat", None),
        P(None, "lat", None),
        P(None, "lat", None),
        P("lat", None),
        P("tm", "lat"),
        P("tm", "lat"),
        P("tm", "lat"),
        P("tm", "lat"),
    )
    return jax.shard_map(
        functools.partial(shards, mesh.shape["tm"], mesh.shape["lat"]),
        mesh=mesh,
        in_specs=placed,
        out_specs=(P("tm", None, "lat", None), P("tm", None, "lat", None), P()),
        check_vma=False,
    )
```

```python
import functools

import jax
import jax.numpy as jnp
from jax import lax
from jax.experimental import pallas as pl
from jax.experimental.pallas import tpu as pltpu
from jax.sharding import PartitionSpec as P

STEPS = 4
ITERS = 2
TILE_LAT = 4
TILE_LON = 16

TIME_STEP = 0.25
MEAN_DEPTH = 1.0
DRAG_RATE = 0.02
STEP_LENGTH = 0.3
CORIOLIS_MEAN = 0.3
CORIOLIS_SLOPE = 0.2
EPSILON = 1e-06

MESH = pl.DeviceIdType.MESH
LANES = 128
DIRECT_MAX = 64
KERNEL_VMEM = 24 * 2**20
WRITE_VMEM = 2**20


def split3(x):
    hi = x.astype(jnp.bfloat16)
    rest = x - hi.astype(jnp.float32)
    mid = rest.astype(jnp.bfloat16)
    low = (rest - mid.astype(jnp.float32)).astype(jnp.bfloat16)
    return jnp.concatenate([hi, mid, low], axis=0)


def join3(y):
    n = y.shape[0] // 3
    return (y[2 * n :] + y[n : 2 * n]) + y[:n]


def fold_lanes(x):
    total = x[:, :LANES]
    for c in range(LANES, x.shape[1], LANES):
        total = total + x[:, c : c + LANES]
    return jnp.sum(total, axis=0, keepdims=True)


def kernel(
    n_tm, n_lat,
    states_hbm, background_hbm, error_hbm, mask_hbm, cells_hbm, moments_hbm, values_hbm, obs_err_hbm,
    est_out, slid_out, costs_out,
    xs, deriv, lam, pack, whole, onehot, obs, gain, cor, masks, variance, inv_var,
    xnext, fe_prev, adj_in, adj_col, dirs, dir_edge, dir_next, parts, parts_tm,
    slid_base, est_dir, slid_dir,
    land_mask, obs_cells, obs_moments, obs_values, obs_error,
    ssem, rsem, lsem, known,
):
    tm = lax.axis_index("tm")
    lat = lax.axis_index("lat")
    rows, cols = variance.shape[1], variance.shape[2]
    lon = whole.shape[2]
    full = gain.shape[1]
    wide = 2 * rows
    half = STEPS
    total_rows = rows * n_lat
    cell_count = 3 * total_rows * lon
    n_dev = n_tm * n_lat
    n_pair = n_tm // 2
    me = tm * n_lat + lat
    side = lax.rem(tm, 2)
    mate = 1 - side
    pair = lax.div(tm, 2)
    even = side == 0
    odd = side == 1
    has_up = lat > 0
    has_down = lat < n_lat - 1
    has_prev = pair > 0
    has_next = pair < n_pair - 1
    is_last = pair == n_pair - 1
    across_tm = tm + 1 - 2 * side
    up = {"lat": lat - 1}
    down = {"lat": lat + 1}
    across = {"tm": across_tm}
    across_up = {"tm": across_tm, "lat": lat - 1}
    across_down = {"tm": across_tm, "lat": lat + 1}
    before = {"tm": tm - 2}
    after = {"tm": tm + 2}
    left = {"tm": tm - 1}
    right = {"tm": tm + 1}
    direct = n_dev <= DIRECT_MAX

    def wrapped(i, n):
        return jnp.where(i >= n, i - n, i)

    lats = [lat] + [wrapped(lat + d, n_lat) for d in range(1, n_lat)]
    tms = [tm] + [wrapped(tm + d, n_tm) for d in range(1, n_tm)]
    lat_partners = [{"lat": lats[d]} for d in range(1, n_lat)]
    tm_partners = [{"tm": tms[d]} for d in range(1, n_tm)]
    if direct:
        pairs = [(t, d) for t in range(n_tm) for d in range(n_lat) if t or d]
        if n_tm & (n_tm - 1) == 0 and n_lat & (n_lat - 1) == 0:
            pairs.sort(key=lambda p: -(p[0] // 2 + p[0] % 2 + p[1] // 2 + 0.1 * (p[1] % 2)))
            all_partners = [
                {"tm": jnp.bitwise_xor(tm, t), "lat": jnp.bitwise_xor(lat, d)} for t, d in pairs
            ]
        else:
            all_partners = [{"tm": tms[t], "lat": lats[d]} for t, d in pairs]

    def guarded(cond, action):
        if cond is None:
            action()
        else:
            pl.when(cond)(action)

    barrier = pltpu.get_barrier_semaphore()
    greeted = [(None, p) for p in lat_partners]
    greeted += [(None, {"tm": across_tm, "lat": lats[d]}) for d in range(n_lat)]
    greeted += [
        (has_prev, before), (has_next, after), (even & has_prev, left), (odd & has_next, right),
    ]
    for cond, partner in greeted:
        guarded(cond, lambda partner=partner: pl.semaphore_signal(
            barrier, inc=1, device_id=partner, device_id_type=MESH))
    reaches = []
    while 2 ** len(reaches) < n_pair:
        reaches.append(2 ** len(reaches))

    def tell(stage):
        d = reaches[stage]
        for cond, target in ((pair >= d, tm - 2 * d), (pair + d < n_pair, tm + 2 * d)):
            @pl.when(cond)
            def _(target=target):
                pl.semaphore_signal(
                    known.at[stage], inc=1, device_id={"tm": target}, device_id_type=MESH
                )

    def hear(stage):
        d = reaches[stage]
        pl.semaphore_wait(
            known.at[stage],
            (pair >= d).astype(jnp.int32) + (pair + d < n_pair).astype(jnp.int32),
        )

    own = slice(0, rows)
    mine = slice(0, cols)
    edge = slice(cols, full)
    loads = []
    my_cols = pl.ds(pl.multiple_of(side * cols, LANES), cols)

    def load(src, dst):
        copy = pltpu.make_async_copy(src, dst, lsem.at[len(loads)])
        copy.start()
        loads.append(copy)

    load(states_hbm.at[0], whole)
    load(mask_hbm, land_mask)
    load(cells_hbm, obs_cells)
    load(moments_hbm, obs_moments)
    load(values_hbm, obs_values)
    load(obs_err_hbm, obs_error)
    load(error_hbm.at[:, :, my_cols], variance)
    for it in range(ITERS):
        @pl.when(pair == 0)
        def _(it=it):
            pltpu.make_async_copy(
                background_hbm.at[:, :, my_cols], fe_prev.at[it], lsem.at[7 + it]
            ).start()

    def remote(src, dst, k, device):
        return pltpu.make_async_remote_copy(
            src_ref=src, dst_ref=dst, send_sem=ssem.at[k], recv_sem=rsem.at[k],
            device_id=device, device_id_type=MESH,
        )

    pending = []
    late = []

    def send(cond, src, dst, k, device, queue=pending):
        guarded(cond, lambda: remote(src, dst, k, device).start())
        queue.append((cond, src, k, device))

    def drain(queue):
        for cond, src, k, device in queue:
            guarded(cond, lambda src=src, k=k, device=device: remote(src, src, k, device).wait_send())
        queue.clear()

    def arrive(cond, dst, k, device):
        guarded(cond, lambda: remote(dst, dst, k, device).wait_recv())

    lo, hi = slice(0, half), slice(half, rows)
    lo_w, hi_w = slice(rows, rows + half), slice(rows + half, wide)

    @pl.when(lat == n_lat - 1)
    def _():
        xs[0, :, :, lo_w] = jnp.zeros((2, 3, half, full), jnp.float32)
        masks[lo_w, :] = jnp.zeros((half, LANES), jnp.float32)
        for it in range(ITERS):
            adj_in[it, :, :, hi] = jnp.zeros((2, 3, half, full), jnp.float32)
            dirs[it, :, :, lo_w] = jnp.zeros((2, 3, half, full), jnp.float32)

    @pl.when(lat == 0)
    def _():
        xs[0, :, :, hi_w] = jnp.zeros((2, 3, half, full), jnp.float32)
        masks[hi_w, :] = jnp.zeros((half, LANES), jnp.float32)
        for it in range(ITERS):
            adj_in[it, :, :, lo] = jnp.zeros((2, 3, half, full), jnp.float32)
            dirs[it, :, :, hi_w] = jnp.zeros((2, 3, half, full), jnp.float32)

    @pl.when(is_last)
    def _():
        xnext[...] = jnp.zeros(xnext.shape, jnp.float32)
        for it in range(ITERS):
            dir_next[it] = jnp.zeros(xnext.shape, jnp.float32)

    loads[1].wait()
    mask = land_mask[...].astype(jnp.float32)
    tile_cols = mask.shape[1]
    masks[own, :] = jnp.concatenate(
        [jnp.broadcast_to(mask[i : i + 1], (TILE_LAT, tile_cols)) for i in range(rows // TILE_LAT)],
        axis=0,
    )

    lane = lax.broadcasted_iota(jnp.int32, (rows, LANES), 1)
    first_lanes = lane < half
    last_lanes = lane >= LANES - half

    def border(first, last):
        return jnp.where(first_lanes, first, jnp.where(last_lanes, last, 0.0))

    loads[0].wait()
    for h in range(2):
        for f in range(3):
            c, o = h * cols, (1 - h) * cols
            pack[h, f, :, mine] = whole[f, :, c : c + cols]
            pack[h, f, :, edge] = border(
                whole[f, :, o : o + LANES], whole[f, :, o + cols - LANES : o + cols]
            )
    pl.semaphore_wait(
        barrier,
        2 * n_lat - 1 + has_prev.astype(jnp.int32) + has_next.astype(jnp.int32)
        + (even & has_prev).astype(jnp.int32) + (odd & has_next).astype(jnp.int32),
    )

    send(has_up, masks.at[lo], masks.at[lo_w], 0, up)
    send(has_down, masks.at[hi], masks.at[hi_w], 1, down)
    send(None, pack.at[mate], xs.at[0, side, :, own], 2, across)
    send(has_up, pack.at[mate, :, lo], xs.at[0, side, :, lo_w], 3, across_up)
    send(has_down, pack.at[mate, :, hi], xs.at[0, side, :, hi_w], 4, across_down)
    send(has_up, pack.at[side, :, lo], xs.at[0, side, :, lo_w], 5, up)
    send(has_down, pack.at[side, :, hi], xs.at[0, side, :, hi_w], 6, down)
    for copy in loads[2:6]:
        copy.wait()
    n_obs = obs_cells.shape[1]
    obs[side] = jnp.concatenate(
        [
            obs_cells[...].astype(jnp.float32), obs_moments[...].astype(jnp.float32),
            obs_values[...], obs_error[...], jnp.zeros((4, n_obs), jnp.float32),
        ],
        axis=0,
    )
    send(None, obs.at[side], obs.at[side], 7, across)
    send(even & has_prev, pack.at[0, :, :, mine], xnext, 8, before)
    send(even & has_prev, pack.at[1, :, :, mine], xnext, 9, left)
    if reaches:
        tell(0)

    xs[0, side, :, own] = pack[side]
    loads[6].wait()
    var = variance[...] * variance[...]
    variance[...] = var
    inv_var[...] = 1.0 / var
    r_id = lax.broadcasted_iota(jnp.int32, (wide, LANES), 0)
    r_id = jnp.where(r_id < rows + half, r_id, r_id - wide) + lat * rows
    cor[...] = 2.0 * (CORIOLIS_MEAN + CORIOLIS_SLOPE * (r_id.astype(jnp.float32) / total_rows - 0.5))
    first_col = lax.broadcasted_iota(jnp.int32, (tile_cols, full), 0) * TILE_LON
    place = lax.broadcasted_iota(jnp.int32, (tile_cols, full), 1)
    col = jnp.where(place < cols + half, place, place - full) + side * cols
    col = jnp.where(col >= lon, col - lon, jnp.where(col < 0, col + lon, col))
    used = (place < cols + half) | (place >= full - half)
    grow = (used & (col >= first_col) & (col < first_col + TILE_LON)).astype(jnp.float32).astype(jnp.bfloat16)

    arrive(None, obs.at[mate], 7, across)
    valid, taken, targets, precision = [], [], [], []
    for w in range(2):
        cells = obs[w, 0:1].astype(jnp.int32)
        cell_row = jnp.zeros_like(cells)
        for r in range(1, rows):
            cell_row = cell_row + (cells >= r * lon).astype(jnp.int32)
        cell_col = cells - cell_row * lon - side * cols
        inside = (cell_col >= 0) & (cell_col < cols)
        onehot[w] = (
            lax.broadcasted_iota(jnp.int32, (cols, n_obs), 0) == cell_col
        ).astype(jnp.float32).astype(jnp.bfloat16)
        valid.append(inside.astype(jnp.float32))
        taken.append((
            (lax.broadcasted_iota(jnp.int32, (STEPS * rows, n_obs), 0)
             == obs[w, 1:2].astype(jnp.int32) * rows + cell_row) & inside
        ).astype(jnp.float32))
        targets.append(obs[w, 2:3])
        precision.append(1.0 / (obs[w, 3:4] * obs[w, 3:4]))

    arrive(has_down, masks.at[lo_w], 0, down)
    arrive(has_up, masks.at[hi_w], 1, up)
    gain[...] = (0.5 * TIME_STEP) * jnp.dot(
        masks[...].astype(jnp.bfloat16), grow, preferred_element_type=jnp.float32,
    )
    arrive(None, xs.at[0, mate, :, own], 2, across)
    arrive(has_down, xs.at[0, mate, :, lo_w], 3, across_down)
    arrive(has_up, xs.at[0, mate, :, hi_w], 4, across_up)
    arrive(has_down, xs.at[0, side, :, lo_w], 5, down)
    arrive(has_up, xs.at[0, side, :, hi_w], 6, up)
    if len(reaches) > 1:
        hear(0)
        tell(1)

    def east(a):
        return pltpu.roll(a, full - 1, 1)

    def west(a):
        return pltpu.roll(a, 1, 1)

    def north(a):
        return pltpu.roll(a, wide - 1, 0)

    def south(a):
        return pltpu.roll(a, 1, 0)

    def dx2(a):
        return east(a) - west(a)

    def dy2(a):
        return north(a) - south(a)

    def coriolis2(n):
        return jnp.concatenate([cor[0:n]] * (full // LANES), axis=-1)

    def forward_step(s, w, n):
        h, u, v = xs[s, w, 0] + MEAN_DEPTH, xs[s, w, 1], xs[s, w, 2]
        h_n, h_s, u_n, u_s = north(h)[:n], south(h)[:n], north(u)[:n], south(u)[:n]
        v_n, v_s = north(v)[:n], south(v)[:n]
        h, u, v = h[:n], u[:n], v[:n]
        h_e, h_w, u_e, u_w, v_e, v_w = east(h), west(h), east(u), west(u), east(v), west(v)
        g = gain[0:n]
        f2 = coriolis2(n)
        drag_u = (u_e - u_w) + 2.0 * DRAG_RATE
        turn_u = f2 - (u_n - u_s)
        turn_v = f2 + (v_e - v_w)
        drag_v = (v_n - v_s) + 2.0 * DRAG_RATE
        xs[s + 1, w, 0, 0:n] = xs[s, w, 0, 0:n] - g * ((h_e * u_e - h_w * u_w) + (h_n * v_n - h_s * v_s))
        xs[s + 1, w, 1, 0:n] = u + g * (v * turn_u - u * drag_u - (h_e - h_w))
        xs[s + 1, w, 2, 0:n] = v - g * (u * turn_v + v * drag_v + (h_n - h_s))
        return drag_u, turn_u, turn_v, drag_v

    def forward(windows, keep):
        for s in range(STEPS):
            n = rows if s == STEPS - 1 else wide
            for w in windows:
                terms = forward_step(s, w, n)
                if keep:
                    for i, term in enumerate(terms):
                        deriv[s, w, i, 0:n] = term

    def padded(a):
        return jnp.concatenate([a, jnp.zeros((rows, full), jnp.float32)], axis=0)

    def edged(a):
        return jnp.concatenate([a, jnp.zeros((a.shape[0], LANES), jnp.float32)], axis=1)

    def adjoint_last(w, closing, forcing):
        s = STEPS - 1
        g = gain[own]
        top = [edged(c) for c in closing]
        a, b, c = top[0] * g, top[1] * g, top[2] * g
        h, u, v = xs[s, w, 0] + MEAN_DEPTH, xs[s, w, 1, own], xs[s, w, 2]
        b_all, c_all = padded(b), padded(c)
        ax, ay, cy = dx2(a), dy2(padded(a)), dy2(c_all)
        vb, vc = dy2(v * b_all), dy2(v * c_all)
        v_ay, h_ay = v * ay, h * ay
        lam[s, w, 0, own] = top[0] + edged(forcing) + u * ax + v_ay[:rows] + dx2(b) + cy[:rows]
        lam[s, w, 0, rows:wide] = v_ay[rows:] + cy[rows:]
        lam[s, w, 1, own] = (
            top[1] + h[:rows] * ax + dx2(u * b) + vb[:rows]
            - b * deriv[s, w, 0, own] - c * deriv[s, w, 2, own]
        )
        lam[s, w, 1, rows:wide] = vb[rows:]
        lam[s, w, 2, own] = (
            top[2] + h_ay[:rows] + dx2(u * c) + vc[:rows]
            + b * deriv[s, w, 1, own] - c * deriv[s, w, 3, own]
        )
        lam[s, w, 2, rows:wide] = h_ay[rows:] + vc[rows:]

    def adjoint_step(s, w, forcing):
        g = gain[...]
        lh, lu, lv = lam[s + 1, w, 0], lam[s + 1, w, 1], lam[s + 1, w, 2]
        a, b, c = lh * g, lu * g, lv * g
        h, u, v = xs[s, w, 0] + MEAN_DEPTH, xs[s, w, 1], xs[s, w, 2]
        ax, ay = dx2(a), dy2(a)
        b_e, b_w, u_e, u_w = east(b), west(b), east(u), west(u)
        c_n, c_s, v_n, v_s = north(c), south(c), north(v), south(v)
        new_h = lh + u * ax + v * ay + (b_e - b_w) + (c_n - c_s)
        lam[s, w, 0, own] = new_h[:rows] + edged(forcing)
        lam[s, w, 0, rows:wide] = new_h[rows:]
        lam[s, w, 1] = (
            lu + h * ax + (u_e * b_e - u_w * b_w) + dy2(v * b)
            - b * deriv[s, w, 0] - c * deriv[s, w, 2]
        )
        lam[s, w, 2] = (
            lv + h * ay + dx2(u * c) + (v_n * c_n - v_s * c_s)
            + b * deriv[s, w, 1] - c * deriv[s, w, 3]
        )

    def exchange(buf, value, k, mine_at, partner):
        buf[mine_at] = value
        for device in partner:
            remote(buf.at[mine_at], buf.at[mine_at], k, device).start()

    def collect(buf, k, size, partner):
        remote(buf.at[0 : size - 1], buf.at[0 : size - 1], k, partner[0]).wait_recv()
        return jnp.sum(buf[...], axis=0)

    def sent(buf, k, size, partner):
        remote(buf.at[0 : size - 1], buf.at[0 : size - 1], k, partner[0]).wait_send()

    scale = None
    scales = []
    est_k = [28 + 14 * ITERS + it for it in range(ITERS)]
    for it in range(ITERS):
        base = 10 + 13 * it
        last = it == ITERS - 1
        forward((0, 1), True)
        send(has_next, xs.at[STEPS, 1, :, own, mine], fe_prev.at[it], base, after)

        misfits, weights, spreads = [], [], []
        for w in range(2):
            heights = jnp.concatenate([xs[s, w, 0, own, mine] for s in range(STEPS)], axis=0)
            seen = join3(
                jnp.dot(split3(heights), onehot[w], preferred_element_type=jnp.float32)
            )
            misfit = jnp.sum(seen * taken[w], axis=0, keepdims=True) - targets[w] * valid[w]
            weighted = misfit * precision[w]
            spreads.append(join3(
                lax.dot_general(
                    split3(taken[w] * weighted), onehot[w], (((1,), (1,)), ((), ())),
                    preferred_element_type=jnp.float32,
                )
            ))
            misfits.append(misfit)
            weights.append(weighted)

        if it == 0:
            arrive(even & has_next, xnext, 8, after)
            arrive(odd & has_next, xnext, 9, right)
            for stage in range(1, len(reaches)):
                hear(stage)
                if stage + 1 < len(reaches):
                    tell(stage + 1)
            if len(reaches) == 1:
                hear(0)
        else:
            arrive(has_next, dir_next.at[it - 1], base - 13 + 11, after)
            xnext[...] = xnext[...] - scale * dir_next[it - 1]
        def forcing(s, w):
            return spreads[w][s * rows : (s + 1) * rows]

        def state(s, w, f):
            return xs[s, w, f, own, mine]

        closings = [
            [(state(STEPS, 0, f) - state(0, 1, f)) * inv_var[f] for f in range(3)],
            [jnp.where(has_next, (state(STEPS, 1, f) - xnext[f]) * inv_var[f], 0.0) for f in range(3)],
        ]
        for w in range(2):
            adjoint_last(w, closings[w], forcing(STEPS - 1, w))
        for s in reversed(range(STEPS - 1)):
            for w in range(2):
                adjoint_step(s, w, forcing(s, w))
        send(has_down, lam.at[0, :, :, lo_w, mine], adj_in.at[it, :, :, lo, mine], base + 1, down)
        send(has_up, lam.at[0, :, :, hi_w, mine], adj_in.at[it, :, :, hi, mine], base + 2, up)
        send(None, lam.at[0, :, :, own, edge], adj_col.at[it], base + 3, across)
        send(has_down, lam.at[0, :, :, lo_w, edge], adj_in.at[it, :, :, lo, edge], base + 4, across_down)
        send(has_up, lam.at[0, :, :, hi_w, edge], adj_in.at[it, :, :, hi, edge], base + 5, across_up)

        if last:
            send(odd, xs.at[0, 1, :, own, mine], slid_base, base + 14, across)
            send(even & has_next, xnext, slid_base, base + 14, across)
        arrive(has_prev, fe_prev.at[it], base, before)

        @pl.when(pair == 0)
        def _():
            pltpu.make_async_copy(
                background_hbm.at[:, :, my_cols], fe_prev.at[it], lsem.at[7 + it]
            ).wait()

        cost = misfits[0] * weights[0] + misfits[1] * weights[1]
        for w in range(2):
            for f in range(3):
                start = fe_prev[it, f] if w == 0 else state(STEPS, 0, f)
                gap = state(0, w, f) - start
                cost = cost + fold_lanes(gap * gap * inv_var[f])
                dirs[it, w, f, own, mine] = gap + variance[f] * lam[0, w, f, own, mine]
        arrive(has_up, adj_in.at[it, :, :, lo, mine], base + 1, up)
        arrive(has_down, adj_in.at[it, :, :, hi, mine], base + 2, down)
        arrive(None, adj_col.at[it], base + 3, across)
        arrive(has_up, adj_in.at[it, :, :, lo, edge], base + 4, across_up)
        arrive(has_down, adj_in.at[it, :, :, hi, edge], base + 5, across_down)
        steep = jnp.zeros((1, LANES), jnp.float32)
        zeros_mid = jnp.zeros((rows, cols - 2 * LANES), jnp.float32)
        for w in range(2):
            for f in range(3):
                sides = adj_in[it, w, f, :, edge] + adj_col[it, w, f]
                extra = jnp.concatenate(
                    [
                        jnp.where(first_lanes, sides, 0.0), zeros_mid,
                        jnp.where(last_lanes, sides, 0.0),
                    ],
                    axis=1,
                )
                direction = dirs[it, w, f, own, mine] + variance[f] * (
                    adj_in[it, w, f, :, mine] + extra
                )
                dirs[it, w, f, own, mine] = direction
                steep = steep + fold_lanes(direction * direction * inv_var[f])
                dir_edge[it, w, f] = border(direction[:, :LANES], direction[:, cols - LANES :])

        message = jnp.concatenate([steep, cost], axis=0)
        if direct:
            exchange(parts.at[it], message, base + 12, me, all_partners)
        else:
            exchange(parts.at[it], message, base + 12, lat, lat_partners)
        go_up, go_down, go = (has_up & is_last, has_down & is_last, is_last) if last else (has_up, has_down, None)
        send(go_up, dirs.at[it, :, :, lo, mine], dirs.at[it, :, :, lo_w, mine], base + 6, up, late)
        send(go_down, dirs.at[it, :, :, hi, mine], dirs.at[it, :, :, hi_w, mine], base + 7, down, late)
        send(go, dir_edge.at[it], dirs.at[it, :, :, own, edge], base + 8, across, late)
        send(go_up, dir_edge.at[it, :, :, lo], dirs.at[it, :, :, lo_w, edge], base + 9, across_up, late)
        send(go_down, dir_edge.at[it, :, :, hi], dirs.at[it, :, :, hi_w, edge], base + 10, across_down, late)

        def send_on():
            if last:
                send(None, dirs.at[it, mate, :, own, mine], est_dir.at[it], est_k[it], across, late)
                send(odd, dirs.at[it, 1, :, own, mine], slid_dir, base + 16, across, late)
                send(even & has_prev, dirs.at[it, 0, :, own, mine], slid_dir, base + 17, left, late)
                send(odd & has_prev, dirs.at[it, 0, :, own, mine], dir_next.at[it], base + 11, before, late)
            else:
                send(has_prev, dirs.at[it, 0, :, own, mine], dir_next.at[it], base + 11, before, late)
                send(None, dirs.at[it, mate, :, own, mine], est_dir.at[it], est_k[it], across, late)
            drain(pending)

        if direct:
            send_on()
            total = collect(parts.at[it], base + 12, n_dev, all_partners)
        else:
            total = collect(parts.at[it], base + 12, n_lat, lat_partners)
            k_tm = 28 + 13 * ITERS + it
            exchange(parts_tm.at[it], total, k_tm, tm, tm_partners)
            send_on()
            total = collect(parts_tm.at[it], k_tm, n_tm, tm_partners)
        steepness = jnp.sum(total[0:1], axis=1, keepdims=True)
        scale = STEP_LENGTH / jnp.sqrt(steepness / (n_tm * cell_count) + EPSILON)
        scales.append(scale)
        costs_out[it : it + 1] = jnp.broadcast_to(
            jnp.sum(total[1:2], axis=1, keepdims=True) * (0.5 / cell_count), (1, LANES)
        )

        for w in range(2):
            for f in range(3):
                xs[0, w, f, own, mine] = state(0, w, f) - scale * dirs[it, w, f, own, mine]
        arrive(go if not last else is_last, dirs.at[it, :, :, own, edge], base + 8, across)
        arrive(go_down, dirs.at[it, :, :, lo_w, mine], base + 6, down)
        arrive(go_up, dirs.at[it, :, :, hi_w, mine], base + 7, up)
        arrive(go_down, dirs.at[it, :, :, lo_w, edge], base + 9, across_down)
        arrive(go_up, dirs.at[it, :, :, hi_w, edge], base + 10, across_up)

        def halos(it=it, windows=(1,) if last else (0, 1), scale=scale):
            for w in windows:
                for f in range(3):
                    xs[0, w, f, own, edge] = xs[0, w, f, own, edge] - scale * dirs[it, w, f, own, edge]
                    xs[0, w, f, rows:wide] = xs[0, w, f, rows:wide] - scale * dirs[it, w, f, rows:wide]

        guarded(is_last if last else None, halos)

    end = 10 + 13 * (ITERS - 1)
    k_end = end + 18

    @pl.when(is_last)
    def _():
        forward((1,), False)

    send(even & is_last, xs.at[STEPS, 1, :, own, mine], slid_dir, k_end, across, late)

    for h in range(2):
        c, o = slice(h * cols, (h + 1) * cols), slice((1 - h) * cols, (2 - h) * cols)

        @pl.when(side == h)
        def _(h=h, c=c):
            est_out[0, :, :, c] = xs[0, h, :, own, mine]
            if h == 0:
                slid_out[0, :, :, c] = xs[0, 1, :, own, mine]

    arrive(even, slid_base, end + 14, across)
    arrive(odd & has_next, slid_base, end + 14, across)
    for it in range(ITERS):
        arrive(None, est_dir.at[it], est_k[it], across)
    moved = [scales[it] * est_dir[it] for it in range(ITERS)]
    for h in range(2):
        o = slice((1 - h) * cols, (2 - h) * cols)

        @pl.when(side == h)
        def _(o=o):
            other = whole[:, :, o]
            for it in range(ITERS):
                other = other - moved[it]
            est_out[0, :, :, o] = other

    arrive(even, slid_dir, end + 16, across)
    arrive(odd & has_next, slid_dir, end + 17, right)
    arrive(odd & has_next, dir_next.at[ITERS - 1], end + 11, after)
    arrive(odd & is_last, slid_dir, k_end, across)

    @pl.when(even)
    def _():
        slid_out[0, :, :, cols:] = slid_base[...] - scale * slid_dir[...]

    @pl.when(odd & has_next)
    def _():
        slid_out[0, :, :, 0:cols] = slid_base[...] - scale * slid_dir[...]
        slid_out[0, :, :, cols:] = xnext[...] - scale * dir_next[ITERS - 1]

    @pl.when(odd & is_last)
    def _():
        slid_out[0, :, :, 0:cols] = slid_dir[...]
        slid_out[0, :, :, cols:] = xs[STEPS, 1, :, own, mine]

    drain(late)
    for it in range(ITERS):
        base = 10 + 13 * it
        if direct:
            sent(parts.at[it], base + 12, n_dev, all_partners)
        else:
            sent(parts.at[it], base + 12, n_lat, lat_partners)
            sent(parts_tm.at[it], 28 + 13 * ITERS + it, n_tm, tm_partners)


def write_out(est, slid, costs, est_out, slid_out, costs_out, held, sem):
    moves = [
        pltpu.make_async_copy(est, est_out, sem.at[0]),
        pltpu.make_async_copy(slid, slid_out, sem.at[1]),
        pltpu.make_async_copy(held, costs_out, sem.at[2]),
    ]
    moves[0].start()
    moves[1].start()
    for it in range(ITERS):
        held[it] = costs[it, 0]
    moves[2].start()
    for copy in moves:
        copy.wait()


def shards(n_tm, n_lat, *args):
    states, background = args[0], args[1]
    _, rows, lon = background.shape
    n_obs = args[4].shape[1]
    wide, cols = 2 * rows, lon // 2
    full = cols + LANES
    f32 = jnp.float32
    direct = n_tm * n_lat <= DIRECT_MAX
    field = (3, rows, cols)
    edge = (2, 3, rows, LANES)
    sems = 28 + 15 * ITERS
    est, slid, costs = pl.pallas_call(
        functools.partial(kernel, n_tm, n_lat),
        out_shape=(
            pltpu.VMEM(states.shape, f32),
            pltpu.VMEM(states.shape, f32),
            pltpu.VMEM((ITERS, LANES), f32),
        ),
        in_specs=[pl.BlockSpec(memory_space=pltpu.HBM)] * 8,
        out_specs=(pl.BlockSpec(memory_space=pltpu.VMEM),) * 3,
        scratch_shapes=[
            pltpu.VMEM((STEPS + 1, 2, 3, wide, full), f32),
            pltpu.VMEM((STEPS, 2, 4, wide, full), f32),
            pltpu.VMEM((STEPS, 2, 3, wide, full), f32),
            pltpu.VMEM((2, 3, rows, full), f32),
            pltpu.VMEM((3, rows, lon), f32),
            pltpu.VMEM((2, cols, n_obs), jnp.bfloat16),
            pltpu.VMEM((2, 8, n_obs), f32),
            pltpu.VMEM((wide, full), f32),
            pltpu.VMEM((wide, LANES), f32),
            pltpu.VMEM((wide, LANES), f32),
            pltpu.VMEM(field, f32),
            pltpu.VMEM(field, f32),
            pltpu.VMEM(field, f32),
            pltpu.VMEM((ITERS,) + field, f32),
            pltpu.VMEM((ITERS, 2, 3, rows, full), f32),
            pltpu.VMEM((ITERS,) + edge, f32),
            pltpu.VMEM((ITERS, 2, 3, wide, full), f32),
            pltpu.VMEM((ITERS,) + edge, f32),
            pltpu.VMEM((ITERS,) + field, f32),
            pltpu.VMEM((ITERS, n_tm * n_lat if direct else n_lat, 2, LANES), f32),
            pltpu.VMEM((ITERS, n_tm, 2, LANES), f32),
            pltpu.VMEM(field, f32),
            pltpu.VMEM((ITERS,) + field, f32),
            pltpu.VMEM(field, f32),
            pltpu.VMEM(args[3].shape, jnp.int32),
            pltpu.VMEM((1, n_obs), jnp.int32),
            pltpu.VMEM((1, n_obs), jnp.int32),
            pltpu.VMEM((1, n_obs), f32),
            pltpu.VMEM((1, n_obs), f32),
            pltpu.SemaphoreType.DMA((sems,)),
            pltpu.SemaphoreType.DMA((sems,)),
            pltpu.SemaphoreType.DMA((7 + ITERS,)),
            pltpu.SemaphoreType.REGULAR((max(n_tm.bit_length(), 1),)),
        ],
        compiler_params=pltpu.CompilerParams(
            collective_id=0, has_side_effects=True, vmem_limit_bytes=KERNEL_VMEM
        ),
    )(*[pltpu.with_memory_space_constraint(a, pltpu.HBM) for a in args])
    return pl.pallas_call(
        write_out,
        out_shape=(
            jax.ShapeDtypeStruct(states.shape, f32),
            jax.ShapeDtypeStruct(states.shape, f32),
            jax.ShapeDtypeStruct((ITERS,), f32),
        ),
        in_specs=[pl.BlockSpec(memory_space=pltpu.VMEM)] * 3,
        out_specs=(pl.BlockSpec(memory_space=pltpu.HBM),) * 3,
        scratch_shapes=[pltpu.SMEM((ITERS,), f32), pltpu.SemaphoreType.DMA((3,))],
        compiler_params=pltpu.CompilerParams(vmem_limit_bytes=WRITE_VMEM),
    )(est, slid, costs)


def solution(mesh):
    placed = (
        P("tm", None, "lat", None),
        P(None, "lat", None),
        P(None, "lat", None),
        P("lat", None),
        P("tm", "lat"),
        P("tm", "lat"),
        P("tm", "lat"),
        P("tm", "lat"),
    )
    return jax.shard_map(
        functools.partial(shards, mesh.shape["tm"], mesh.shape["lat"]),
        mesh=mesh,
        in_specs=placed,
        out_specs=(P("tm", None, "lat", None), P("tm", None, "lat", None), P()),
        check_vma=False,
    )
```

```python
import functools

import jax
import jax.numpy as jnp
from jax import lax
from jax.experimental import pallas as pl
from jax.experimental.pallas import tpu as pltpu
from jax.sharding import PartitionSpec as P

STEPS = 4
ITERS = 2
TILE_LAT = 4
TILE_LON = 16

TIME_STEP = 0.25
MEAN_DEPTH = 1.0
DRAG_RATE = 0.02
STEP_LENGTH = 0.3
CORIOLIS_MEAN = 0.3
CORIOLIS_SLOPE = 0.2
EPSILON = 1e-06

MESH = pl.DeviceIdType.MESH
LANES = 128
DIRECT_MAX = 64
KERNEL_VMEM = 24 * 2**20
WRITE_VMEM = 2**20


def split3(x):
    hi = x.astype(jnp.bfloat16)
    rest = x - hi.astype(jnp.float32)
    mid = rest.astype(jnp.bfloat16)
    low = (rest - mid.astype(jnp.float32)).astype(jnp.bfloat16)
    return jnp.concatenate([hi, mid, low], axis=0)


def join3(y):
    n = y.shape[0] // 3
    return (y[2 * n :] + y[n : 2 * n]) + y[:n]


def fold_lanes(x):
    total = x[:, :LANES]
    for c in range(LANES, x.shape[1], LANES):
        total = total + x[:, c : c + LANES]
    return jnp.sum(total, axis=0, keepdims=True)


def kernel(
    n_tm, n_lat,
    states_hbm, background_hbm, error_hbm, mask_hbm, cells_hbm, moments_hbm, values_hbm, obs_err_hbm,
    est_out, slid_out, costs_out,
    xs, deriv, lam, pack, whole, onehot, obs, gain, cor, masks, variance, inv_var,
    xnext, fe_prev, adj_in, adj_col, dirs, dir_edge, dir_next, parts, parts_tm,
    slid_base, est_dir, slid_dir,
    land_mask, obs_cells, obs_moments, obs_values, obs_error,
    ssem, rsem, lsem, known,
):
    tm = lax.axis_index("tm")
    lat = lax.axis_index("lat")
    rows, cols = variance.shape[1], variance.shape[2]
    lon = whole.shape[2]
    full = gain.shape[1]
    wide = 2 * rows
    half = STEPS
    total_rows = rows * n_lat
    cell_count = 3 * total_rows * lon
    n_dev = n_tm * n_lat
    n_pair = n_tm // 2
    me = tm * n_lat + lat
    side = lax.rem(tm, 2)
    mate = 1 - side
    pair = lax.div(tm, 2)
    even = side == 0
    odd = side == 1
    has_up = lat > 0
    has_down = lat < n_lat - 1
    has_prev = pair > 0
    has_next = pair < n_pair - 1
    is_last = pair == n_pair - 1
    core = lax.rem(lat, 2)
    up_far, down_near = has_up & (core == 0), has_down & (core == 0)
    up_near, down_far = has_up & (core == 1), has_down & (core == 1)
    across_tm = tm + 1 - 2 * side
    up = {"lat": lat - 1}
    down = {"lat": lat + 1}
    across = {"tm": across_tm}
    across_up = {"tm": across_tm, "lat": lat - 1}
    across_down = {"tm": across_tm, "lat": lat + 1}
    before = {"tm": tm - 2}
    after = {"tm": tm + 2}
    left = {"tm": tm - 1}
    right = {"tm": tm + 1}
    direct = n_dev <= DIRECT_MAX

    def wrapped(i, n):
        return jnp.where(i >= n, i - n, i)

    lats = [lat] + [wrapped(lat + d, n_lat) for d in range(1, n_lat)]
    tms = [tm] + [wrapped(tm + d, n_tm) for d in range(1, n_tm)]
    lat_partners = [{"lat": lats[d]} for d in range(1, n_lat)]
    tm_partners = [{"tm": tms[d]} for d in range(1, n_tm)]
    if direct:
        pairs = [(t, d) for t in range(n_tm) for d in range(n_lat) if t or d]
        if n_tm & (n_tm - 1) == 0 and n_lat & (n_lat - 1) == 0:
            pairs.sort(key=lambda p: -(p[0] // 2 + p[0] % 2 + p[1] // 2 + 0.1 * (p[1] % 2)))
            all_partners = [
                {"tm": jnp.bitwise_xor(tm, t), "lat": jnp.bitwise_xor(lat, d)} for t, d in pairs
            ]
        else:
            all_partners = [{"tm": tms[t], "lat": lats[d]} for t, d in pairs]

    def guarded(cond, action):
        if cond is None:
            action()
        else:
            pl.when(cond)(action)

    barrier = pltpu.get_barrier_semaphore()
    greeted = [(None, p) for p in lat_partners]
    greeted += [(None, {"tm": across_tm, "lat": lats[d]}) for d in range(n_lat)]
    greeted += [
        (has_prev, before), (has_next, after), (even & has_prev, left), (odd & has_next, right),
    ]
    for cond, partner in greeted:
        guarded(cond, lambda partner=partner: pl.semaphore_signal(
            barrier, inc=1, device_id=partner, device_id_type=MESH))
    reaches = []
    while 2 ** len(reaches) < n_pair:
        reaches.append(2 ** len(reaches))

    def tell(stage):
        d = reaches[stage]
        for cond, target in ((pair >= d, tm - 2 * d), (pair + d < n_pair, tm + 2 * d)):
            @pl.when(cond)
            def _(target=target):
                pl.semaphore_signal(
                    known.at[stage], inc=1, device_id={"tm": target}, device_id_type=MESH
                )

    def hear(stage):
        d = reaches[stage]
        pl.semaphore_wait(
            known.at[stage],
            (pair >= d).astype(jnp.int32) + (pair + d < n_pair).astype(jnp.int32),
        )

    own = slice(0, rows)
    mine = slice(0, cols)
    edge = slice(cols, full)
    loads = []
    my_cols = pl.ds(pl.multiple_of(side * cols, LANES), cols)

    def load(src, dst):
        copy = pltpu.make_async_copy(src, dst, lsem.at[len(loads)])
        copy.start()
        loads.append(copy)

    load(states_hbm.at[0], whole)
    load(mask_hbm, land_mask)
    load(cells_hbm, obs_cells)
    load(moments_hbm, obs_moments)
    load(values_hbm, obs_values)
    load(obs_err_hbm, obs_error)
    load(error_hbm.at[:, :, my_cols], variance)
    for it in range(ITERS):
        @pl.when(pair == 0)
        def _(it=it):
            pltpu.make_async_copy(
                background_hbm.at[:, :, my_cols], fe_prev.at[it], lsem.at[7 + it]
            ).start()

    def remote(src, dst, k, device):
        return pltpu.make_async_remote_copy(
            src_ref=src, dst_ref=dst, send_sem=ssem.at[k], recv_sem=rsem.at[k],
            device_id=device, device_id_type=MESH,
        )

    pending = []
    late = []

    def send(cond, src, dst, k, device, queue=pending):
        guarded(cond, lambda: remote(src, dst, k, device).start())
        queue.append((cond, src, k, device))

    def drain(queue):
        for cond, src, k, device in queue:
            guarded(cond, lambda src=src, k=k, device=device: remote(src, src, k, device).wait_send())
        queue.clear()

    def arrive(cond, dst, k, device):
        guarded(cond, lambda: remote(dst, dst, k, device).wait_recv())

    lo, hi = slice(0, half), slice(half, rows)
    lo_w, hi_w = slice(rows, rows + half), slice(rows + half, wide)

    @pl.when(lat == n_lat - 1)
    def _():
        xs[0, :, :, lo_w] = jnp.zeros((2, 3, half, full), jnp.float32)
        masks[lo_w, :] = jnp.zeros((half, LANES), jnp.float32)
        for it in range(ITERS):
            adj_in[it, :, :, hi] = jnp.zeros((2, 3, half, full), jnp.float32)
            dirs[it, :, :, lo_w] = jnp.zeros((2, 3, half, full), jnp.float32)

    @pl.when(lat == 0)
    def _():
        xs[0, :, :, hi_w] = jnp.zeros((2, 3, half, full), jnp.float32)
        masks[hi_w, :] = jnp.zeros((half, LANES), jnp.float32)
        for it in range(ITERS):
            adj_in[it, :, :, lo] = jnp.zeros((2, 3, half, full), jnp.float32)
            dirs[it, :, :, hi_w] = jnp.zeros((2, 3, half, full), jnp.float32)

    @pl.when(is_last)
    def _():
        xnext[...] = jnp.zeros(xnext.shape, jnp.float32)
        for it in range(ITERS):
            dir_next[it] = jnp.zeros(xnext.shape, jnp.float32)

    loads[1].wait()
    mask = land_mask[...].astype(jnp.float32)
    tile_cols = mask.shape[1]
    masks[own, :] = jnp.concatenate(
        [jnp.broadcast_to(mask[i : i + 1], (TILE_LAT, tile_cols)) for i in range(rows // TILE_LAT)],
        axis=0,
    )

    lane = lax.broadcasted_iota(jnp.int32, (rows, LANES), 1)
    first_lanes = lane < half
    last_lanes = lane >= LANES - half

    def border(first, last):
        return jnp.where(first_lanes, first, jnp.where(last_lanes, last, 0.0))

    loads[0].wait()
    for h in range(2):
        for f in range(3):
            c, o = h * cols, (1 - h) * cols
            pack[h, f, :, mine] = whole[f, :, c : c + cols]
            pack[h, f, :, edge] = border(
                whole[f, :, o : o + LANES], whole[f, :, o + cols - LANES : o + cols]
            )
    for copy in loads[2:6]:
        copy.wait()
    n_obs = obs_cells.shape[1]
    obs[side] = jnp.concatenate(
        [
            obs_cells[...].astype(jnp.float32), obs_moments[...].astype(jnp.float32),
            obs_values[...], obs_error[...], jnp.zeros((4, n_obs), jnp.float32),
        ],
        axis=0,
    )
    pl.semaphore_wait(
        barrier,
        2 * n_lat - 1 + has_prev.astype(jnp.int32) + has_next.astype(jnp.int32)
        + (even & has_prev).astype(jnp.int32) + (odd & has_next).astype(jnp.int32),
    )

    send(has_up, masks.at[lo], masks.at[lo_w], 0, up)
    send(has_down, masks.at[hi], masks.at[hi_w], 1, down)
    send(None, obs.at[side], obs.at[side], 7, across)
    send(has_up, pack.at[side, :, lo], xs.at[0, side, :, lo_w], 5, up)
    send(has_down, pack.at[side, :, hi], xs.at[0, side, :, hi_w], 6, down)
    send(None, pack.at[mate], xs.at[0, side, :, own], 2, across)
    send(up_far, pack.at[mate, :, lo], xs.at[0, side, :, lo_w], 3, across_up)
    send(down_far, pack.at[mate, :, hi], xs.at[0, side, :, hi_w], 4, across_down)
    send(even & has_prev, pack.at[0, :, :, mine], xnext, 8, before)
    send(even & has_prev, pack.at[1, :, :, mine], xnext, 9, left)
    if reaches:
        tell(0)

    xs[0, side, :, own] = pack[side]
    loads[6].wait()
    var = variance[...] * variance[...]
    variance[...] = var
    inv_var[...] = 1.0 / var
    r_id = lax.broadcasted_iota(jnp.int32, (wide, LANES), 0)
    r_id = jnp.where(r_id < rows + half, r_id, r_id - wide) + lat * rows
    cor[...] = 2.0 * (CORIOLIS_MEAN + CORIOLIS_SLOPE * (r_id.astype(jnp.float32) / total_rows - 0.5))
    first_col = lax.broadcasted_iota(jnp.int32, (tile_cols, full), 0) * TILE_LON
    place = lax.broadcasted_iota(jnp.int32, (tile_cols, full), 1)
    col = jnp.where(place < cols + half, place, place - full) + side * cols
    col = jnp.where(col >= lon, col - lon, jnp.where(col < 0, col + lon, col))
    used = (place < cols + half) | (place >= full - half)
    grow = (used & (col >= first_col) & (col < first_col + TILE_LON)).astype(jnp.float32).astype(jnp.bfloat16)

    arrive(None, obs.at[mate], 7, across)
    valid, taken, targets, precision = [], [], [], []
    for w in range(2):
        cells = obs[w, 0:1].astype(jnp.int32)
        cell_row = jnp.zeros_like(cells)
        for r in range(1, rows):
            cell_row = cell_row + (cells >= r * lon).astype(jnp.int32)
        cell_col = cells - cell_row * lon - side * cols
        inside = (cell_col >= 0) & (cell_col < cols)
        onehot[w] = (
            lax.broadcasted_iota(jnp.int32, (cols, n_obs), 0) == cell_col
        ).astype(jnp.float32).astype(jnp.bfloat16)
        valid.append(inside.astype(jnp.float32))
        taken.append((
            (lax.broadcasted_iota(jnp.int32, (STEPS * rows, n_obs), 0)
             == obs[w, 1:2].astype(jnp.int32) * rows + cell_row) & inside
        ).astype(jnp.float32))
        targets.append(obs[w, 2:3])
        precision.append(1.0 / (obs[w, 3:4] * obs[w, 3:4]))

    arrive(has_down, masks.at[lo_w], 0, down)
    arrive(has_up, masks.at[hi_w], 1, up)
    gain[...] = (0.5 * TIME_STEP) * jnp.dot(
        masks[...].astype(jnp.bfloat16), grow, preferred_element_type=jnp.float32,
    )
    arrive(has_down, xs.at[0, side, :, lo_w], 5, down)
    arrive(has_up, xs.at[0, side, :, hi_w], 6, up)

    def east(a):
        return pltpu.roll(a, full - 1, 1)

    def west(a):
        return pltpu.roll(a, 1, 1)

    def north(a):
        return pltpu.roll(a, wide - 1, 0)

    def south(a):
        return pltpu.roll(a, 1, 0)

    def dx2(a):
        return east(a) - west(a)

    def dy2(a):
        return north(a) - south(a)

    def coriolis2(n):
        return jnp.concatenate([cor[0:n]] * (full // LANES), axis=-1)

    def forward_step(s, w, n):
        h, u, v = xs[s, w, 0] + MEAN_DEPTH, xs[s, w, 1], xs[s, w, 2]
        h_n, h_s, u_n, u_s = north(h)[:n], south(h)[:n], north(u)[:n], south(u)[:n]
        v_n, v_s = north(v)[:n], south(v)[:n]
        h, u, v = h[:n], u[:n], v[:n]
        h_e, h_w, u_e, u_w, v_e, v_w = east(h), west(h), east(u), west(u), east(v), west(v)
        g = gain[0:n]
        f2 = coriolis2(n)
        drag_u = (u_e - u_w) + 2.0 * DRAG_RATE
        turn_u = f2 - (u_n - u_s)
        turn_v = f2 + (v_e - v_w)
        drag_v = (v_n - v_s) + 2.0 * DRAG_RATE
        xs[s + 1, w, 0, 0:n] = xs[s, w, 0, 0:n] - g * ((h_e * u_e - h_w * u_w) + (h_n * v_n - h_s * v_s))
        xs[s + 1, w, 1, 0:n] = u + g * (v * turn_u - u * drag_u - (h_e - h_w))
        xs[s + 1, w, 2, 0:n] = v - g * (u * turn_v + v * drag_v + (h_n - h_s))
        return drag_u, turn_u, turn_v, drag_v

    def forward(windows, keep):
        for s in range(STEPS):
            n = rows if s == STEPS - 1 else wide
            for w in windows:
                terms = forward_step(s, w, n)
                if keep:
                    for i, term in enumerate(terms):
                        deriv[s, w, i, 0:n] = term

    def padded(a):
        return jnp.concatenate([a, jnp.zeros((rows, full), jnp.float32)], axis=0)

    def edged(a):
        return jnp.concatenate([a, jnp.zeros((a.shape[0], LANES), jnp.float32)], axis=1)

    def adjoint_last(w, closing, forcing):
        s = STEPS - 1
        g = gain[own]
        top = [edged(c) for c in closing]
        a, b, c = top[0] * g, top[1] * g, top[2] * g
        h, u, v = xs[s, w, 0] + MEAN_DEPTH, xs[s, w, 1, own], xs[s, w, 2]
        b_all, c_all = padded(b), padded(c)
        ax, ay, cy = dx2(a), dy2(padded(a)), dy2(c_all)
        vb, vc = dy2(v * b_all), dy2(v * c_all)
        v_ay, h_ay = v * ay, h * ay
        lam[s, w, 0, own] = top[0] + edged(forcing) + u * ax + v_ay[:rows] + dx2(b) + cy[:rows]
        lam[s, w, 0, rows:wide] = v_ay[rows:] + cy[rows:]
        lam[s, w, 1, own] = (
            top[1] + h[:rows] * ax + dx2(u * b) + vb[:rows]
            - b * deriv[s, w, 0, own] - c * deriv[s, w, 2, own]
        )
        lam[s, w, 1, rows:wide] = vb[rows:]
        lam[s, w, 2, own] = (
            top[2] + h_ay[:rows] + dx2(u * c) + vc[:rows]
            + b * deriv[s, w, 1, own] - c * deriv[s, w, 3, own]
        )
        lam[s, w, 2, rows:wide] = h_ay[rows:] + vc[rows:]

    def adjoint_step(s, w, forcing):
        g = gain[...]
        lh, lu, lv = lam[s + 1, w, 0], lam[s + 1, w, 1], lam[s + 1, w, 2]
        a, b, c = lh * g, lu * g, lv * g
        h, u, v = xs[s, w, 0] + MEAN_DEPTH, xs[s, w, 1], xs[s, w, 2]
        ax, ay = dx2(a), dy2(a)
        b_e, b_w, u_e, u_w = east(b), west(b), east(u), west(u)
        c_n, c_s, v_n, v_s = north(c), south(c), north(v), south(v)
        new_h = lh + u * ax + v * ay + (b_e - b_w) + (c_n - c_s)
        lam[s, w, 0, own] = new_h[:rows] + edged(forcing)
        lam[s, w, 0, rows:wide] = new_h[rows:]
        lam[s, w, 1] = (
            lu + h * ax + (u_e * b_e - u_w * b_w) + dy2(v * b)
            - b * deriv[s, w, 0] - c * deriv[s, w, 2]
        )
        lam[s, w, 2] = (
            lv + h * ay + dx2(u * c) + (v_n * c_n - v_s * c_s)
            + b * deriv[s, w, 1] - c * deriv[s, w, 3]
        )

    def exchange(buf, value, k, mine_at, partner):
        buf[mine_at] = value
        for device in partner:
            remote(buf.at[mine_at], buf.at[mine_at], k, device).start()

    def collect(buf, k, size, partner):
        remote(buf.at[0 : size - 1], buf.at[0 : size - 1], k, partner[0]).wait_recv()
        return jnp.sum(buf[...], axis=0)

    def sent(buf, k, size, partner):
        remote(buf.at[0 : size - 1], buf.at[0 : size - 1], k, partner[0]).wait_send()

    scale = None
    scales = []
    est_k = [28 + 14 * ITERS + it for it in range(ITERS)]
    for it in range(ITERS):
        base = 10 + 13 * it
        last = it == ITERS - 1
        if it == 0:
            forward((side,), True)
            arrive(None, xs.at[0, mate, :, own], 2, across)
            k_near = 28 + 15 * ITERS
            send(up_near, xs.at[0, mate, :, lo], xs.at[0, mate, :, lo_w], k_near, up)
            send(down_near, xs.at[0, mate, :, hi], xs.at[0, mate, :, hi_w], k_near + 1, down)
            arrive(down_far, xs.at[0, mate, :, lo_w], 3, across_down)
            arrive(up_far, xs.at[0, mate, :, hi_w], 4, across_up)
            arrive(down_near, xs.at[0, mate, :, lo_w], k_near, down)
            arrive(up_near, xs.at[0, mate, :, hi_w], k_near + 1, up)
            if len(reaches) > 1:
                hear(0)
                tell(1)
            forward((mate,), True)
        else:
            forward((0, 1), True)
        send(has_next, xs.at[STEPS, 1, :, own, mine], fe_prev.at[it], base, after)

        misfits, weights, spreads = [], [], []
        for w in range(2):
            heights = jnp.concatenate([xs[s, w, 0, own, mine] for s in range(STEPS)], axis=0)
            seen = join3(
                jnp.dot(split3(heights), onehot[w], preferred_element_type=jnp.float32)
            )
            misfit = jnp.sum(seen * taken[w], axis=0, keepdims=True) - targets[w] * valid[w]
            weighted = misfit * precision[w]
            spreads.append(join3(
                lax.dot_general(
                    split3(taken[w] * weighted), onehot[w], (((1,), (1,)), ((), ())),
                    preferred_element_type=jnp.float32,
                )
            ))
            misfits.append(misfit)
            weights.append(weighted)

        if it == 0:
            arrive(even & has_next, xnext, 8, after)
            arrive(odd & has_next, xnext, 9, right)
            for stage in range(1, len(reaches)):
                hear(stage)
                if stage + 1 < len(reaches):
                    tell(stage + 1)
            if len(reaches) == 1:
                hear(0)
        else:
            arrive(has_next, dir_next.at[it - 1], base - 13 + 11, after)
            xnext[...] = xnext[...] - scale * dir_next[it - 1]
        def forcing(s, w):
            return spreads[w][s * rows : (s + 1) * rows]

        def state(s, w, f):
            return xs[s, w, f, own, mine]

        closings = [
            [(state(STEPS, 0, f) - state(0, 1, f)) * inv_var[f] for f in range(3)],
            [jnp.where(has_next, (state(STEPS, 1, f) - xnext[f]) * inv_var[f], 0.0) for f in range(3)],
        ]
        for w in range(2):
            adjoint_last(w, closings[w], forcing(STEPS - 1, w))
        for s in reversed(range(STEPS - 1)):
            for w in range(2):
                adjoint_step(s, w, forcing(s, w))
        send(has_down, lam.at[0, :, :, lo_w, mine], adj_in.at[it, :, :, lo, mine], base + 1, down)
        send(has_up, lam.at[0, :, :, hi_w, mine], adj_in.at[it, :, :, hi, mine], base + 2, up)
        send(None, lam.at[0, :, :, own, edge], adj_col.at[it], base + 3, across)
        send(has_down, lam.at[0, :, :, lo_w, edge], adj_in.at[it, :, :, lo, edge], base + 4, across_down)
        send(has_up, lam.at[0, :, :, hi_w, edge], adj_in.at[it, :, :, hi, edge], base + 5, across_up)

        if last:
            send(odd, xs.at[0, 1, :, own, mine], slid_base, base + 14, across)
            send(even & has_next, xnext, slid_base, base + 14, across)
        arrive(has_prev, fe_prev.at[it], base, before)

        @pl.when(pair == 0)
        def _():
            pltpu.make_async_copy(
                background_hbm.at[:, :, my_cols], fe_prev.at[it], lsem.at[7 + it]
            ).wait()

        cost = misfits[0] * weights[0] + misfits[1] * weights[1]
        for w in range(2):
            for f in range(3):
                start = fe_prev[it, f] if w == 0 else state(STEPS, 0, f)
                gap = state(0, w, f) - start
                cost = cost + fold_lanes(gap * gap * inv_var[f])
                dirs[it, w, f, own, mine] = gap + variance[f] * lam[0, w, f, own, mine]
        arrive(has_up, adj_in.at[it, :, :, lo, mine], base + 1, up)
        arrive(has_down, adj_in.at[it, :, :, hi, mine], base + 2, down)
        arrive(None, adj_col.at[it], base + 3, across)
        arrive(has_up, adj_in.at[it, :, :, lo, edge], base + 4, across_up)
        arrive(has_down, adj_in.at[it, :, :, hi, edge], base + 5, across_down)
        steep = jnp.zeros((1, LANES), jnp.float32)
        zeros_mid = jnp.zeros((rows, cols - 2 * LANES), jnp.float32)
        for w in range(2):
            for f in range(3):
                sides = adj_in[it, w, f, :, edge] + adj_col[it, w, f]
                extra = jnp.concatenate(
                    [
                        jnp.where(first_lanes, sides, 0.0), zeros_mid,
                        jnp.where(last_lanes, sides, 0.0),
                    ],
                    axis=1,
                )
                direction = dirs[it, w, f, own, mine] + variance[f] * (
                    adj_in[it, w, f, :, mine] + extra
                )
                dirs[it, w, f, own, mine] = direction
                steep = steep + fold_lanes(direction * direction * inv_var[f])
                dir_edge[it, w, f] = border(direction[:, :LANES], direction[:, cols - LANES :])

        message = jnp.concatenate([steep, cost], axis=0)
        if last:
            send(None, dirs.at[it, mate, 0:1, own, mine], est_dir.at[it, 0:1], est_k[it], across, late)
        if direct:
            exchange(parts.at[it], message, base + 12, me, all_partners)
        else:
            exchange(parts.at[it], message, base + 12, lat, lat_partners)
        go_up, go_down, go = (has_up & is_last, has_down & is_last, is_last) if last else (has_up, has_down, None)
        send(go_up, dirs.at[it, :, :, lo, mine], dirs.at[it, :, :, lo_w, mine], base + 6, up, late)
        send(go_down, dirs.at[it, :, :, hi, mine], dirs.at[it, :, :, hi_w, mine], base + 7, down, late)
        send(go, dir_edge.at[it], dirs.at[it, :, :, own, edge], base + 8, across, late)
        send(go_up, dir_edge.at[it, :, :, lo], dirs.at[it, :, :, lo_w, edge], base + 9, across_up, late)
        send(go_down, dir_edge.at[it, :, :, hi], dirs.at[it, :, :, hi_w, edge], base + 10, across_down, late)

        def send_on():
            if last:
                send(None, dirs.at[it, mate, 1:3, own, mine], est_dir.at[it, 1:3], base + 13, across, late)
                send(odd, dirs.at[it, 1, :, own, mine], slid_dir, base + 16, across, late)
                send(even & has_prev, dirs.at[it, 0, :, own, mine], slid_dir, base + 17, left, late)
                send(odd & has_prev, dirs.at[it, 0, :, own, mine], dir_next.at[it], base + 11, before, late)
            else:
                send(has_prev, dirs.at[it, 0, :, own, mine], dir_next.at[it], base + 11, before, late)
                send(None, dirs.at[it, mate, :, own, mine], est_dir.at[it], est_k[it], across, late)
            drain(pending)

        if direct:
            send_on()
            total = collect(parts.at[it], base + 12, n_dev, all_partners)
        else:
            total = collect(parts.at[it], base + 12, n_lat, lat_partners)
            k_tm = 28 + 13 * ITERS + it
            exchange(parts_tm.at[it], total, k_tm, tm, tm_partners)
            send_on()
            total = collect(parts_tm.at[it], k_tm, n_tm, tm_partners)
        steepness = jnp.sum(total[0:1], axis=1, keepdims=True)
        scale = STEP_LENGTH / jnp.sqrt(steepness / (n_tm * cell_count) + EPSILON)
        scales.append(scale)
        costs_out[it : it + 1] = jnp.broadcast_to(
            jnp.sum(total[1:2], axis=1, keepdims=True) * (0.5 / cell_count), (1, LANES)
        )

        for w in range(2):
            for f in range(3):
                xs[0, w, f, own, mine] = state(0, w, f) - scale * dirs[it, w, f, own, mine]
        arrive(go if not last else is_last, dirs.at[it, :, :, own, edge], base + 8, across)
        arrive(go_down, dirs.at[it, :, :, lo_w, mine], base + 6, down)
        arrive(go_up, dirs.at[it, :, :, hi_w, mine], base + 7, up)
        arrive(go_down, dirs.at[it, :, :, lo_w, edge], base + 9, across_down)
        arrive(go_up, dirs.at[it, :, :, hi_w, edge], base + 10, across_up)

        def halos(it=it, windows=(1,) if last else (0, 1), scale=scale):
            for w in windows:
                for f in range(3):
                    xs[0, w, f, own, edge] = xs[0, w, f, own, edge] - scale * dirs[it, w, f, own, edge]
                    xs[0, w, f, rows:wide] = xs[0, w, f, rows:wide] - scale * dirs[it, w, f, rows:wide]

        guarded(is_last if last else None, halos)

    end = 10 + 13 * (ITERS - 1)
    k_end = end + 18

    @pl.when(is_last)
    def _():
        forward((1,), False)

    send(even & is_last, xs.at[STEPS, 1, :, own, mine], slid_dir, k_end, across, late)

    for h in range(2):
        c, o = slice(h * cols, (h + 1) * cols), slice((1 - h) * cols, (2 - h) * cols)

        @pl.when(side == h)
        def _(h=h, c=c):
            est_out[0, :, :, c] = xs[0, h, :, own, mine]
            if h == 0:
                slid_out[0, :, :, c] = xs[0, 1, :, own, mine]

    arrive(even, slid_base, end + 14, across)
    arrive(odd & has_next, slid_base, end + 14, across)
    for it in range(ITERS - 1):
        arrive(None, est_dir.at[it], est_k[it], across)
    arrive(None, est_dir.at[ITERS - 1, 0:1], est_k[ITERS - 1], across)
    arrive(None, est_dir.at[ITERS - 1, 1:3], end + 13, across)
    moved = [scales[it] * est_dir[it] for it in range(ITERS)]
    for h in range(2):
        o = slice((1 - h) * cols, (2 - h) * cols)

        @pl.when(side == h)
        def _(o=o):
            other = whole[:, :, o]
            for it in range(ITERS):
                other = other - moved[it]
            est_out[0, :, :, o] = other

    arrive(even, slid_dir, end + 16, across)
    arrive(odd & has_next, slid_dir, end + 17, right)
    arrive(odd & has_next, dir_next.at[ITERS - 1], end + 11, after)
    arrive(odd & is_last, slid_dir, k_end, across)

    @pl.when(even)
    def _():
        slid_out[0, :, :, cols:] = slid_base[...] - scale * slid_dir[...]

    @pl.when(odd & has_next)
    def _():
        slid_out[0, :, :, 0:cols] = slid_base[...] - scale * slid_dir[...]
        slid_out[0, :, :, cols:] = xnext[...] - scale * dir_next[ITERS - 1]

    @pl.when(odd & is_last)
    def _():
        slid_out[0, :, :, 0:cols] = slid_dir[...]
        slid_out[0, :, :, cols:] = xs[STEPS, 1, :, own, mine]

    drain(late)
    for it in range(ITERS):
        base = 10 + 13 * it
        if direct:
            sent(parts.at[it], base + 12, n_dev, all_partners)
        else:
            sent(parts.at[it], base + 12, n_lat, lat_partners)
            sent(parts_tm.at[it], 28 + 13 * ITERS + it, n_tm, tm_partners)


def write_out(est, slid, costs, est_out, slid_out, costs_out, held, sem):
    moves = [
        pltpu.make_async_copy(est, est_out, sem.at[0]),
        pltpu.make_async_copy(slid, slid_out, sem.at[1]),
        pltpu.make_async_copy(held, costs_out, sem.at[2]),
    ]
    moves[0].start()
    moves[1].start()
    for it in range(ITERS):
        held[it] = costs[it, 0]
    moves[2].start()
    for copy in moves:
        copy.wait()


def shards(n_tm, n_lat, *args):
    states, background = args[0], args[1]
    _, rows, lon = background.shape
    n_obs = args[4].shape[1]
    wide, cols = 2 * rows, lon // 2
    full = cols + LANES
    f32 = jnp.float32
    direct = n_tm * n_lat <= DIRECT_MAX
    field = (3, rows, cols)
    edge = (2, 3, rows, LANES)
    sems = 30 + 15 * ITERS
    est, slid, costs = pl.pallas_call(
        functools.partial(kernel, n_tm, n_lat),
        out_shape=(
            pltpu.VMEM(states.shape, f32),
            pltpu.VMEM(states.shape, f32),
            pltpu.VMEM((ITERS, LANES), f32),
        ),
        in_specs=[pl.BlockSpec(memory_space=pltpu.HBM)] * 8,
        out_specs=(pl.BlockSpec(memory_space=pltpu.VMEM),) * 3,
        scratch_shapes=[
            pltpu.VMEM((STEPS + 1, 2, 3, wide, full), f32),
            pltpu.VMEM((STEPS, 2, 4, wide, full), f32),
            pltpu.VMEM((STEPS, 2, 3, wide, full), f32),
            pltpu.VMEM((2, 3, rows, full), f32),
            pltpu.VMEM((3, rows, lon), f32),
            pltpu.VMEM((2, cols, n_obs), jnp.bfloat16),
            pltpu.VMEM((2, 8, n_obs), f32),
            pltpu.VMEM((wide, full), f32),
            pltpu.VMEM((wide, LANES), f32),
            pltpu.VMEM((wide, LANES), f32),
            pltpu.VMEM(field, f32),
            pltpu.VMEM(field, f32),
            pltpu.VMEM(field, f32),
            pltpu.VMEM((ITERS,) + field, f32),
            pltpu.VMEM((ITERS, 2, 3, rows, full), f32),
            pltpu.VMEM((ITERS,) + edge, f32),
            pltpu.VMEM((ITERS, 2, 3, wide, full), f32),
            pltpu.VMEM((ITERS,) + edge, f32),
            pltpu.VMEM((ITERS,) + field, f32),
            pltpu.VMEM((ITERS, n_tm * n_lat if direct else n_lat, 2, LANES), f32),
            pltpu.VMEM((ITERS, n_tm, 2, LANES), f32),
            pltpu.VMEM(field, f32),
            pltpu.VMEM((ITERS,) + field, f32),
            pltpu.VMEM(field, f32),
            pltpu.VMEM(args[3].shape, jnp.int32),
            pltpu.VMEM((1, n_obs), jnp.int32),
            pltpu.VMEM((1, n_obs), jnp.int32),
            pltpu.VMEM((1, n_obs), f32),
            pltpu.VMEM((1, n_obs), f32),
            pltpu.SemaphoreType.DMA((sems,)),
            pltpu.SemaphoreType.DMA((sems,)),
            pltpu.SemaphoreType.DMA((7 + ITERS,)),
            pltpu.SemaphoreType.REGULAR((max(n_tm.bit_length(), 1),)),
        ],
        compiler_params=pltpu.CompilerParams(
            collective_id=0, has_side_effects=True, vmem_limit_bytes=KERNEL_VMEM
        ),
    )(*[pltpu.with_memory_space_constraint(a, pltpu.HBM) for a in args])
    return pl.pallas_call(
        write_out,
        out_shape=(
            jax.ShapeDtypeStruct(states.shape, f32),
            jax.ShapeDtypeStruct(states.shape, f32),
            jax.ShapeDtypeStruct((ITERS,), f32),
        ),
        in_specs=[pl.BlockSpec(memory_space=pltpu.VMEM)] * 3,
        out_specs=(pl.BlockSpec(memory_space=pltpu.HBM),) * 3,
        scratch_shapes=[pltpu.SMEM((ITERS,), f32), pltpu.SemaphoreType.DMA((3,))],
        compiler_params=pltpu.CompilerParams(vmem_limit_bytes=WRITE_VMEM),
    )(est, slid, costs)


def solution(mesh):
    placed = (
        P("tm", None, "lat", None),
        P(None, "lat", None),
        P(None, "lat", None),
        P("lat", None),
        P("tm", "lat"),
        P("tm", "lat"),
        P("tm", "lat"),
        P("tm", "lat"),
    )
    return jax.shard_map(
        functools.partial(shards, mesh.shape["tm"], mesh.shape["lat"]),
        mesh=mesh,
        in_specs=placed,
        out_specs=(P("tm", None, "lat", None), P("tm", None, "lat", None), P()),
        check_vma=False,
    )
```

```python
import functools

import jax
import jax.numpy as jnp
from jax import lax
from jax.experimental import pallas as pl
from jax.experimental.pallas import tpu as pltpu
from jax.sharding import PartitionSpec as P

STEPS = 4
ITERS = 2
TILE_LAT = 4
TILE_LON = 16

TIME_STEP = 0.25
MEAN_DEPTH = 1.0
DRAG_RATE = 0.02
STEP_LENGTH = 0.3
CORIOLIS_MEAN = 0.3
CORIOLIS_SLOPE = 0.2
EPSILON = 1e-06

MESH = pl.DeviceIdType.MESH
LANES = 128
DIRECT_MAX = 64
KERNEL_VMEM = 24 * 2**20
WRITE_VMEM = 2**20


def split3(x):
    hi = x.astype(jnp.bfloat16)
    rest = x - hi.astype(jnp.float32)
    mid = rest.astype(jnp.bfloat16)
    low = (rest - mid.astype(jnp.float32)).astype(jnp.bfloat16)
    return jnp.concatenate([hi, mid, low], axis=0)


def join3(y):
    n = y.shape[0] // 3
    return (y[2 * n :] + y[n : 2 * n]) + y[:n]


def fold_lanes(x):
    total = x[:, :LANES]
    for c in range(LANES, x.shape[1], LANES):
        total = total + x[:, c : c + LANES]
    return jnp.sum(total, axis=0, keepdims=True)


def kernel(
    n_tm, n_lat,
    states_hbm, background_hbm, error_hbm, mask_hbm, cells_hbm, moments_hbm, values_hbm, obs_err_hbm,
    est_out, slid_out, costs_out,
    xs, deriv, lam, pack, whole, onehot, obs, gain, cor, masks, variance, inv_var,
    xnext, fe_prev, adj_in, adj_col, dirs, dir_edge, dir_next, parts, parts_tm,
    slid_base, est_dir, slid_dir,
    land_mask, obs_cells, obs_moments, obs_values, obs_error,
    ssem, rsem, lsem, known,
):
    tm = lax.axis_index("tm")
    lat = lax.axis_index("lat")
    rows, cols = variance.shape[1], variance.shape[2]
    lon = whole.shape[2]
    full = gain.shape[1]
    wide = 2 * rows
    half = STEPS
    total_rows = rows * n_lat
    cell_count = 3 * total_rows * lon
    n_dev = n_tm * n_lat
    n_pair = n_tm // 2
    me = tm * n_lat + lat
    side = lax.rem(tm, 2)
    mate = 1 - side
    pair = lax.div(tm, 2)
    even = side == 0
    odd = side == 1
    has_up = lat > 0
    has_down = lat < n_lat - 1
    has_prev = pair > 0
    has_next = pair < n_pair - 1
    is_last = pair == n_pair - 1
    core = lax.rem(lat, 2)
    up_far, down_near = has_up & (core == 0), has_down & (core == 0)
    up_near, down_far = has_up & (core == 1), has_down & (core == 1)
    across_tm = tm + 1 - 2 * side
    up = {"lat": lat - 1}
    down = {"lat": lat + 1}
    across = {"tm": across_tm}
    across_up = {"tm": across_tm, "lat": lat - 1}
    across_down = {"tm": across_tm, "lat": lat + 1}
    before = {"tm": tm - 2}
    after = {"tm": tm + 2}
    left = {"tm": tm - 1}
    right = {"tm": tm + 1}
    direct = n_dev <= DIRECT_MAX

    def wrapped(i, n):
        return jnp.where(i >= n, i - n, i)

    lats = [lat] + [wrapped(lat + d, n_lat) for d in range(1, n_lat)]
    tms = [tm] + [wrapped(tm + d, n_tm) for d in range(1, n_tm)]
    lat_partners = [{"lat": lats[d]} for d in range(1, n_lat)]
    tm_partners = [{"tm": tms[d]} for d in range(1, n_tm)]
    if direct:
        pairs = [(t, d) for t in range(n_tm) for d in range(n_lat) if t or d]
        if n_tm & (n_tm - 1) == 0 and n_lat & (n_lat - 1) == 0:
            pairs.sort(key=lambda p: -(p[0] // 2 + p[0] % 2 + p[1] // 2 + 0.1 * (p[1] % 2)))
            all_partners = [
                {"tm": jnp.bitwise_xor(tm, t), "lat": jnp.bitwise_xor(lat, d)} for t, d in pairs
            ]
        else:
            all_partners = [{"tm": tms[t], "lat": lats[d]} for t, d in pairs]

    def guarded(cond, action):
        if cond is None:
            action()
        else:
            pl.when(cond)(action)

    barrier = pltpu.get_barrier_semaphore()
    greeted = [(None, p) for p in lat_partners]
    greeted += [(None, {"tm": across_tm, "lat": lats[d]}) for d in range(n_lat)]
    greeted += [
        (has_prev, before), (has_next, after), (even & has_prev, left), (odd & has_next, right),
    ]
    for cond, partner in greeted:
        guarded(cond, lambda partner=partner: pl.semaphore_signal(
            barrier, inc=1, device_id=partner, device_id_type=MESH))
    reaches = []
    while 2 ** len(reaches) < n_pair:
        reaches.append(2 ** len(reaches))

    def tell(stage):
        d = reaches[stage]
        for cond, target in ((pair >= d, tm - 2 * d), (pair + d < n_pair, tm + 2 * d)):
            @pl.when(cond)
            def _(target=target):
                pl.semaphore_signal(
                    known.at[stage], inc=1, device_id={"tm": target}, device_id_type=MESH
                )

    def hear(stage):
        d = reaches[stage]
        pl.semaphore_wait(
            known.at[stage],
            (pair >= d).astype(jnp.int32) + (pair + d < n_pair).astype(jnp.int32),
        )

    own = slice(0, rows)
    mine = slice(0, cols)
    edge = slice(cols, full)
    loads = []
    my_cols = pl.ds(pl.multiple_of(side * cols, LANES), cols)

    def load(src, dst):
        copy = pltpu.make_async_copy(src, dst, lsem.at[len(loads)])
        copy.start()
        loads.append(copy)

    load(states_hbm.at[0], whole)
    load(mask_hbm, land_mask)
    load(cells_hbm, obs_cells)
    load(moments_hbm, obs_moments)
    load(values_hbm, obs_values)
    load(obs_err_hbm, obs_error)
    load(error_hbm.at[:, :, my_cols], variance)
    for it in range(ITERS):
        @pl.when(pair == 0)
        def _(it=it):
            pltpu.make_async_copy(
                background_hbm.at[:, :, my_cols], fe_prev.at[it], lsem.at[7 + it]
            ).start()

    def remote(src, dst, k, device):
        return pltpu.make_async_remote_copy(
            src_ref=src, dst_ref=dst, send_sem=ssem.at[k], recv_sem=rsem.at[k],
            device_id=device, device_id_type=MESH,
        )

    pending = []
    late = []

    def send(cond, src, dst, k, device, queue=pending):
        guarded(cond, lambda: remote(src, dst, k, device).start())
        queue.append((cond, src, k, device))

    def drain(queue):
        for cond, src, k, device in queue:
            guarded(cond, lambda src=src, k=k, device=device: remote(src, src, k, device).wait_send())
        queue.clear()

    def arrive(cond, dst, k, device):
        guarded(cond, lambda: remote(dst, dst, k, device).wait_recv())

    lo, hi = slice(0, half), slice(half, rows)
    lo_w, hi_w = slice(rows, rows + half), slice(rows + half, wide)

    @pl.when(lat == n_lat - 1)
    def _():
        xs[0, :, :, lo_w] = jnp.zeros((2, 3, half, full), jnp.float32)
        masks[lo_w, :] = jnp.zeros((half, LANES), jnp.float32)
        for it in range(ITERS):
            adj_in[it, :, :, hi] = jnp.zeros((2, 3, half, full), jnp.float32)
            dirs[it, :, :, lo_w] = jnp.zeros((2, 3, half, full), jnp.float32)

    @pl.when(lat == 0)
    def _():
        xs[0, :, :, hi_w] = jnp.zeros((2, 3, half, full), jnp.float32)
        masks[hi_w, :] = jnp.zeros((half, LANES), jnp.float32)
        for it in range(ITERS):
            adj_in[it, :, :, lo] = jnp.zeros((2, 3, half, full), jnp.float32)
            dirs[it, :, :, hi_w] = jnp.zeros((2, 3, half, full), jnp.float32)

    @pl.when(is_last)
    def _():
        xnext[...] = jnp.zeros(xnext.shape, jnp.float32)
        for it in range(ITERS):
            dir_next[it] = jnp.zeros(xnext.shape, jnp.float32)

    loads[1].wait()
    mask = land_mask[...].astype(jnp.float32)
    tile_cols = mask.shape[1]
    masks[own, :] = jnp.concatenate(
        [jnp.broadcast_to(mask[i : i + 1], (TILE_LAT, tile_cols)) for i in range(rows // TILE_LAT)],
        axis=0,
    )

    lane = lax.broadcasted_iota(jnp.int32, (rows, LANES), 1)
    first_lanes = lane < half
    last_lanes = lane >= LANES - half

    def border(first, last):
        return jnp.where(first_lanes, first, jnp.where(last_lanes, last, 0.0))

    loads[0].wait()
    for h in range(2):
        for f in range(3):
            c, o = h * cols, (1 - h) * cols
            pack[h, f, :, mine] = whole[f, :, c : c + cols]
            pack[h, f, :, edge] = border(
                whole[f, :, o : o + LANES], whole[f, :, o + cols - LANES : o + cols]
            )
    for copy in loads[2:6]:
        copy.wait()
    n_obs = obs_cells.shape[1]
    obs[side] = jnp.concatenate(
        [
            obs_cells[...].astype(jnp.float32), obs_moments[...].astype(jnp.float32),
            obs_values[...], obs_error[...], jnp.zeros((4, n_obs), jnp.float32),
        ],
        axis=0,
    )
    pl.semaphore_wait(
        barrier,
        2 * n_lat - 1 + has_prev.astype(jnp.int32) + has_next.astype(jnp.int32)
        + (even & has_prev).astype(jnp.int32) + (odd & has_next).astype(jnp.int32),
    )

    send(has_up, masks.at[lo], masks.at[lo_w], 0, up)
    send(has_down, masks.at[hi], masks.at[hi_w], 1, down)
    send(None, obs.at[side], obs.at[side], 7, across)
    send(has_up, pack.at[side, :, lo], xs.at[0, side, :, lo_w], 5, up)
    send(has_down, pack.at[side, :, hi], xs.at[0, side, :, hi_w], 6, down)
    send(None, pack.at[mate], xs.at[0, side, :, own], 2, across)
    send(up_far, pack.at[mate, :, lo], xs.at[0, side, :, lo_w], 3, across_up)
    send(down_far, pack.at[mate, :, hi], xs.at[0, side, :, hi_w], 4, across_down)
    send(even & has_prev, pack.at[0, :, :, mine], xnext, 8, before)
    send(even & has_prev, pack.at[1, :, :, mine], xnext, 9, left)
    if reaches:
        tell(0)

    xs[0, side, :, own] = pack[side]
    loads[6].wait()
    var = variance[...] * variance[...]
    variance[...] = var
    inv_var[...] = 1.0 / var
    r_id = lax.broadcasted_iota(jnp.int32, (wide, LANES), 0)
    r_id = jnp.where(r_id < rows + half, r_id, r_id - wide) + lat * rows
    cor[...] = 2.0 * (CORIOLIS_MEAN + CORIOLIS_SLOPE * (r_id.astype(jnp.float32) / total_rows - 0.5))
    first_col = lax.broadcasted_iota(jnp.int32, (tile_cols, full), 0) * TILE_LON
    place = lax.broadcasted_iota(jnp.int32, (tile_cols, full), 1)
    col = jnp.where(place < cols + half, place, place - full) + side * cols
    col = jnp.where(col >= lon, col - lon, jnp.where(col < 0, col + lon, col))
    used = (place < cols + half) | (place >= full - half)
    grow = (used & (col >= first_col) & (col < first_col + TILE_LON)).astype(jnp.float32).astype(jnp.bfloat16)

    arrive(None, obs.at[mate], 7, across)
    valid, taken, targets, precision = [], [], [], []
    for w in range(2):
        cells = obs[w, 0:1].astype(jnp.int32)
        cell_row = jnp.zeros_like(cells)
        for r in range(1, rows):
            cell_row = cell_row + (cells >= r * lon).astype(jnp.int32)
        cell_col = cells - cell_row * lon - side * cols
        inside = (cell_col >= 0) & (cell_col < cols)
        onehot[w] = (
            lax.broadcasted_iota(jnp.int32, (cols, n_obs), 0) == cell_col
        ).astype(jnp.float32).astype(jnp.bfloat16)
        valid.append(inside.astype(jnp.float32))
        taken.append((
            (lax.broadcasted_iota(jnp.int32, (STEPS * rows, n_obs), 0)
             == obs[w, 1:2].astype(jnp.int32) * rows + cell_row) & inside
        ).astype(jnp.float32))
        targets.append(obs[w, 2:3])
        precision.append(1.0 / (obs[w, 3:4] * obs[w, 3:4]))

    arrive(has_down, masks.at[lo_w], 0, down)
    arrive(has_up, masks.at[hi_w], 1, up)
    gain[...] = (0.5 * TIME_STEP) * jnp.dot(
        masks[...].astype(jnp.bfloat16), grow, preferred_element_type=jnp.float32,
    )
    arrive(has_down, xs.at[0, side, :, lo_w], 5, down)
    arrive(has_up, xs.at[0, side, :, hi_w], 6, up)

    def east(a):
        return pltpu.roll(a, full - 1, 1)

    def west(a):
        return pltpu.roll(a, 1, 1)

    def north(a):
        return pltpu.roll(a, wide - 1, 0)

    def south(a):
        return pltpu.roll(a, 1, 0)

    def dx2(a):
        return east(a) - west(a)

    def dy2(a):
        return north(a) - south(a)

    def coriolis2(n):
        return jnp.concatenate([cor[0:n]] * (full // LANES), axis=-1)

    def forward_step(s, w, n):
        h, u, v = xs[s, w, 0] + MEAN_DEPTH, xs[s, w, 1], xs[s, w, 2]
        h_n, h_s, u_n, u_s = north(h)[:n], south(h)[:n], north(u)[:n], south(u)[:n]
        v_n, v_s = north(v)[:n], south(v)[:n]
        h, u, v = h[:n], u[:n], v[:n]
        h_e, h_w, u_e, u_w, v_e, v_w = east(h), west(h), east(u), west(u), east(v), west(v)
        g = gain[0:n]
        f2 = coriolis2(n)
        drag_u = (u_e - u_w) + 2.0 * DRAG_RATE
        turn_u = f2 - (u_n - u_s)
        turn_v = f2 + (v_e - v_w)
        drag_v = (v_n - v_s) + 2.0 * DRAG_RATE
        xs[s + 1, w, 0, 0:n] = xs[s, w, 0, 0:n] - g * ((h_e * u_e - h_w * u_w) + (h_n * v_n - h_s * v_s))
        xs[s + 1, w, 1, 0:n] = u + g * (v * turn_u - u * drag_u - (h_e - h_w))
        xs[s + 1, w, 2, 0:n] = v - g * (u * turn_v + v * drag_v + (h_n - h_s))
        return drag_u, turn_u, turn_v, drag_v

    def forward(windows, keep):
        for s in range(STEPS):
            n = rows if s == STEPS - 1 else wide
            for w in windows:
                terms = forward_step(s, w, n)
                if keep:
                    for i, term in enumerate(terms):
                        deriv[s, w, i, 0:n] = term

    def padded(a):
        return jnp.concatenate([a, jnp.zeros((rows, full), jnp.float32)], axis=0)

    def edged(a):
        return jnp.concatenate([a, jnp.zeros((a.shape[0], LANES), jnp.float32)], axis=1)

    def adjoint_last(w, closing, forcing):
        s = STEPS - 1
        g = gain[own]
        top = [edged(c) for c in closing]
        a, b, c = top[0] * g, top[1] * g, top[2] * g
        h, u, v = xs[s, w, 0] + MEAN_DEPTH, xs[s, w, 1, own], xs[s, w, 2]
        b_all, c_all = padded(b), padded(c)
        ax, ay, cy = dx2(a), dy2(padded(a)), dy2(c_all)
        vb, vc = dy2(v * b_all), dy2(v * c_all)
        v_ay, h_ay = v * ay, h * ay
        lam[s, w, 0, own] = top[0] + edged(forcing) + u * ax + v_ay[:rows] + dx2(b) + cy[:rows]
        lam[s, w, 0, rows:wide] = v_ay[rows:] + cy[rows:]
        lam[s, w, 1, own] = (
            top[1] + h[:rows] * ax + dx2(u * b) + vb[:rows]
            - b * deriv[s, w, 0, own] - c * deriv[s, w, 2, own]
        )
        lam[s, w, 1, rows:wide] = vb[rows:]
        lam[s, w, 2, own] = (
            top[2] + h_ay[:rows] + dx2(u * c) + vc[:rows]
            + b * deriv[s, w, 1, own] - c * deriv[s, w, 3, own]
        )
        lam[s, w, 2, rows:wide] = h_ay[rows:] + vc[rows:]

    def adjoint_step(s, w, forcing):
        g = gain[...]
        lh, lu, lv = lam[s + 1, w, 0], lam[s + 1, w, 1], lam[s + 1, w, 2]
        a, b, c = lh * g, lu * g, lv * g
        h, u, v = xs[s, w, 0] + MEAN_DEPTH, xs[s, w, 1], xs[s, w, 2]
        ax, ay = dx2(a), dy2(a)
        b_e, b_w, u_e, u_w = east(b), west(b), east(u), west(u)
        c_n, c_s, v_n, v_s = north(c), south(c), north(v), south(v)
        new_h = lh + u * ax + v * ay + (b_e - b_w) + (c_n - c_s)
        lam[s, w, 0, own] = new_h[:rows] + edged(forcing)
        lam[s, w, 0, rows:wide] = new_h[rows:]
        lam[s, w, 1] = (
            lu + h * ax + (u_e * b_e - u_w * b_w) + dy2(v * b)
            - b * deriv[s, w, 0] - c * deriv[s, w, 2]
        )
        lam[s, w, 2] = (
            lv + h * ay + dx2(u * c) + (v_n * c_n - v_s * c_s)
            + b * deriv[s, w, 1] - c * deriv[s, w, 3]
        )

    def exchange(buf, value, k, mine_at, partner):
        buf[mine_at] = value
        for device in partner:
            remote(buf.at[mine_at], buf.at[mine_at], k, device).start()

    def collect(buf, k, size, partner):
        remote(buf.at[0 : size - 1], buf.at[0 : size - 1], k, partner[0]).wait_recv()
        return jnp.sum(buf[...], axis=0)

    def sent(buf, k, size, partner):
        remote(buf.at[0 : size - 1], buf.at[0 : size - 1], k, partner[0]).wait_send()

    scale = None
    scales = []
    est_k = [28 + 14 * ITERS + it for it in range(ITERS)]
    for it in range(ITERS):
        base = 10 + 13 * it
        last = it == ITERS - 1
        if it == 0:
            forward((side,), True)
            arrive(None, xs.at[0, mate, :, own], 2, across)
            k_near = 28 + 15 * ITERS
            send(up_near, xs.at[0, mate, :, lo], xs.at[0, mate, :, lo_w], k_near, up)
            send(down_near, xs.at[0, mate, :, hi], xs.at[0, mate, :, hi_w], k_near + 1, down)
            arrive(down_far, xs.at[0, mate, :, lo_w], 3, across_down)
            arrive(up_far, xs.at[0, mate, :, hi_w], 4, across_up)
            arrive(down_near, xs.at[0, mate, :, lo_w], k_near, down)
            arrive(up_near, xs.at[0, mate, :, hi_w], k_near + 1, up)
            if len(reaches) > 1:
                hear(0)
                tell(1)
            forward((mate,), True)
        else:
            forward((1,), True)
        send(has_next, xs.at[STEPS, 1, :, own, mine], fe_prev.at[it], base, after)
        if it > 0:
            forward((0,), True)

        misfits, weights, spreads = [], [], []
        for w in range(2):
            heights = jnp.concatenate([xs[s, w, 0, own, mine] for s in range(STEPS)], axis=0)
            seen = join3(
                jnp.dot(split3(heights), onehot[w], preferred_element_type=jnp.float32)
            )
            misfit = jnp.sum(seen * taken[w], axis=0, keepdims=True) - targets[w] * valid[w]
            weighted = misfit * precision[w]
            spreads.append(join3(
                lax.dot_general(
                    split3(taken[w] * weighted), onehot[w], (((1,), (1,)), ((), ())),
                    preferred_element_type=jnp.float32,
                )
            ))
            misfits.append(misfit)
            weights.append(weighted)

        def forcing(s, w):
            return spreads[w][s * rows : (s + 1) * rows]

        def state(s, w, f):
            return xs[s, w, f, own, mine]

        for w in range(2):
            if w == 0:
                closing = [(state(STEPS, 0, f) - state(0, 1, f)) * inv_var[f] for f in range(3)]
            else:
                if it == 0:
                    arrive(even & has_next, xnext, 8, after)
                    arrive(odd & has_next, xnext, 9, right)
                    for stage in range(1, len(reaches)):
                        hear(stage)
                        if stage + 1 < len(reaches):
                            tell(stage + 1)
                    if len(reaches) == 1:
                        hear(0)
                else:
                    arrive(has_next, dir_next.at[it - 1], base - 13 + 11, after)
                    xnext[...] = xnext[...] - scale * dir_next[it - 1]
                closing = [
                    jnp.where(has_next, (state(STEPS, 1, f) - xnext[f]) * inv_var[f], 0.0)
                    for f in range(3)
                ]
            adjoint_last(w, closing, forcing(STEPS - 1, w))
            for s in reversed(range(STEPS - 1)):
                adjoint_step(s, w, forcing(s, w))
            k = base + 1 if w == 0 else 30 + 15 * ITERS + 5 * it
            send(None, lam.at[0, w, :, own, edge], adj_col.at[it, w], k + 2, across)
            send(has_down, lam.at[0, w, :, lo_w, edge], adj_in.at[it, w, :, lo, edge], k + 3, across_down)
            send(has_up, lam.at[0, w, :, hi_w, edge], adj_in.at[it, w, :, hi, edge], k + 4, across_up)
            send(has_down, lam.at[0, w, :, lo_w, mine], adj_in.at[it, w, :, lo, mine], k, down)
            send(has_up, lam.at[0, w, :, hi_w, mine], adj_in.at[it, w, :, hi, mine], k + 1, up)
        if last:
            send(odd, xs.at[0, 1, :, own, mine], slid_base, base + 14, across)
            send(even & has_next, xnext, slid_base, base + 14, across)
        arrive(has_prev, fe_prev.at[it], base, before)

        @pl.when(pair == 0)
        def _():
            pltpu.make_async_copy(
                background_hbm.at[:, :, my_cols], fe_prev.at[it], lsem.at[7 + it]
            ).wait()

        cost = misfits[0] * weights[0] + misfits[1] * weights[1]
        for w in range(2):
            for f in range(3):
                start = fe_prev[it, f] if w == 0 else state(STEPS, 0, f)
                gap = state(0, w, f) - start
                cost = cost + fold_lanes(gap * gap * inv_var[f])
                dirs[it, w, f, own, mine] = gap + variance[f] * lam[0, w, f, own, mine]
        steep = jnp.zeros((1, LANES), jnp.float32)
        zeros_mid = jnp.zeros((rows, cols - 2 * LANES), jnp.float32)
        for w in range(2):
            k = base + 1 if w == 0 else 30 + 15 * ITERS + 5 * it
            arrive(has_up, adj_in.at[it, w, :, lo, mine], k, up)
            arrive(has_down, adj_in.at[it, w, :, hi, mine], k + 1, down)
            arrive(None, adj_col.at[it, w], k + 2, across)
            arrive(has_up, adj_in.at[it, w, :, lo, edge], k + 3, across_up)
            arrive(has_down, adj_in.at[it, w, :, hi, edge], k + 4, across_down)
            for f in range(3):
                sides = adj_in[it, w, f, :, edge] + adj_col[it, w, f]
                extra = jnp.concatenate(
                    [
                        jnp.where(first_lanes, sides, 0.0), zeros_mid,
                        jnp.where(last_lanes, sides, 0.0),
                    ],
                    axis=1,
                )
                direction = dirs[it, w, f, own, mine] + variance[f] * (
                    adj_in[it, w, f, :, mine] + extra
                )
                dirs[it, w, f, own, mine] = direction
                steep = steep + fold_lanes(direction * direction * inv_var[f])
                dir_edge[it, w, f] = border(direction[:, :LANES], direction[:, cols - LANES :])

        message = jnp.concatenate([steep, cost], axis=0)
        if last:
            send(None, dirs.at[it, mate, 0:1, own, mine], est_dir.at[it, 0:1], est_k[it], across, late)
        if direct:
            exchange(parts.at[it], message, base + 12, me, all_partners)
        else:
            exchange(parts.at[it], message, base + 12, lat, lat_partners)
        go_up, go_down, go = (has_up & is_last, has_down & is_last, is_last) if last else (has_up, has_down, None)
        send(go_up, dirs.at[it, :, :, lo, mine], dirs.at[it, :, :, lo_w, mine], base + 6, up, late)
        send(go_down, dirs.at[it, :, :, hi, mine], dirs.at[it, :, :, hi_w, mine], base + 7, down, late)
        send(go, dir_edge.at[it], dirs.at[it, :, :, own, edge], base + 8, across, late)
        send(go_up, dir_edge.at[it, :, :, lo], dirs.at[it, :, :, lo_w, edge], base + 9, across_up, late)
        send(go_down, dir_edge.at[it, :, :, hi], dirs.at[it, :, :, hi_w, edge], base + 10, across_down, late)

        def send_on():
            if last:
                send(None, dirs.at[it, mate, 1:3, own, mine], est_dir.at[it, 1:3], base + 13, across, late)
                send(odd, dirs.at[it, 1, :, own, mine], slid_dir, base + 16, across, late)
                send(even & has_prev, dirs.at[it, 0, :, own, mine], slid_dir, base + 17, left, late)
                send(odd & has_prev, dirs.at[it, 0, :, own, mine], dir_next.at[it], base + 11, before, late)
            else:
                send(has_prev, dirs.at[it, 0, :, own, mine], dir_next.at[it], base + 11, before, late)
                send(None, dirs.at[it, mate, :, own, mine], est_dir.at[it], est_k[it], across, late)
            drain(pending)

        if direct:
            send_on()
            total = collect(parts.at[it], base + 12, n_dev, all_partners)
        else:
            total = collect(parts.at[it], base + 12, n_lat, lat_partners)
            k_tm = 28 + 13 * ITERS + it
            exchange(parts_tm.at[it], total, k_tm, tm, tm_partners)
            send_on()
            total = collect(parts_tm.at[it], k_tm, n_tm, tm_partners)
        steepness = jnp.sum(total[0:1], axis=1, keepdims=True)
        scale = STEP_LENGTH / jnp.sqrt(steepness / (n_tm * cell_count) + EPSILON)
        scales.append(scale)
        costs_out[it : it + 1] = jnp.broadcast_to(
            jnp.sum(total[1:2], axis=1, keepdims=True) * (0.5 / cell_count), (1, LANES)
        )

        for w in range(2):
            for f in range(3):
                xs[0, w, f, own, mine] = state(0, w, f) - scale * dirs[it, w, f, own, mine]
        arrive(go if not last else is_last, dirs.at[it, :, :, own, edge], base + 8, across)
        arrive(go_down, dirs.at[it, :, :, lo_w, mine], base + 6, down)
        arrive(go_up, dirs.at[it, :, :, hi_w, mine], base + 7, up)
        arrive(go_down, dirs.at[it, :, :, lo_w, edge], base + 9, across_down)
        arrive(go_up, dirs.at[it, :, :, hi_w, edge], base + 10, across_up)

        def halos(it=it, windows=(1,) if last else (0, 1), scale=scale):
            for w in windows:
                for f in range(3):
                    xs[0, w, f, own, edge] = xs[0, w, f, own, edge] - scale * dirs[it, w, f, own, edge]
                    xs[0, w, f, rows:wide] = xs[0, w, f, rows:wide] - scale * dirs[it, w, f, rows:wide]

        guarded(is_last if last else None, halos)

    end = 10 + 13 * (ITERS - 1)
    k_end = end + 18

    @pl.when(is_last)
    def _():
        forward((1,), False)

    send(even & is_last, xs.at[STEPS, 1, :, own, mine], slid_dir, k_end, across, late)

    for h in range(2):
        c, o = slice(h * cols, (h + 1) * cols), slice((1 - h) * cols, (2 - h) * cols)

        @pl.when(side == h)
        def _(h=h, c=c):
            est_out[0, :, :, c] = xs[0, h, :, own, mine]
            if h == 0:
                slid_out[0, :, :, c] = xs[0, 1, :, own, mine]

    arrive(even, slid_base, end + 14, across)
    arrive(odd & has_next, slid_base, end + 14, across)
    for it in range(ITERS - 1):
        arrive(None, est_dir.at[it], est_k[it], across)
    arrive(None, est_dir.at[ITERS - 1, 0:1], est_k[ITERS - 1], across)
    arrive(None, est_dir.at[ITERS - 1, 1:3], end + 13, across)
    moved = [scales[it] * est_dir[it] for it in range(ITERS)]
    for h in range(2):
        o = slice((1 - h) * cols, (2 - h) * cols)

        @pl.when(side == h)
        def _(o=o):
            other = whole[:, :, o]
            for it in range(ITERS):
                other = other - moved[it]
            est_out[0, :, :, o] = other

    arrive(even, slid_dir, end + 16, across)
    arrive(odd & has_next, slid_dir, end + 17, right)
    arrive(odd & has_next, dir_next.at[ITERS - 1], end + 11, after)
    arrive(odd & is_last, slid_dir, k_end, across)

    @pl.when(even)
    def _():
        slid_out[0, :, :, cols:] = slid_base[...] - scale * slid_dir[...]

    @pl.when(odd & has_next)
    def _():
        slid_out[0, :, :, 0:cols] = slid_base[...] - scale * slid_dir[...]
        slid_out[0, :, :, cols:] = xnext[...] - scale * dir_next[ITERS - 1]

    @pl.when(odd & is_last)
    def _():
        slid_out[0, :, :, 0:cols] = slid_dir[...]
        slid_out[0, :, :, cols:] = xs[STEPS, 1, :, own, mine]

    drain(late)
    for it in range(ITERS):
        base = 10 + 13 * it
        if direct:
            sent(parts.at[it], base + 12, n_dev, all_partners)
        else:
            sent(parts.at[it], base + 12, n_lat, lat_partners)
            sent(parts_tm.at[it], 28 + 13 * ITERS + it, n_tm, tm_partners)


def write_out(est, slid, costs, est_out, slid_out, costs_out, held, sem):
    moves = [
        pltpu.make_async_copy(est, est_out, sem.at[0]),
        pltpu.make_async_copy(slid, slid_out, sem.at[1]),
        pltpu.make_async_copy(held, costs_out, sem.at[2]),
    ]
    moves[0].start()
    moves[1].start()
    for it in range(ITERS):
        held[it] = costs[it, 0]
    moves[2].start()
    for copy in moves:
        copy.wait()


def shards(n_tm, n_lat, *args):
    states, background = args[0], args[1]
    _, rows, lon = background.shape
    n_obs = args[4].shape[1]
    wide, cols = 2 * rows, lon // 2
    full = cols + LANES
    f32 = jnp.float32
    direct = n_tm * n_lat <= DIRECT_MAX
    field = (3, rows, cols)
    edge = (2, 3, rows, LANES)
    sems = 30 + 20 * ITERS
    est, slid, costs = pl.pallas_call(
        functools.partial(kernel, n_tm, n_lat),
        out_shape=(
            pltpu.VMEM(states.shape, f32),
            pltpu.VMEM(states.shape, f32),
            pltpu.VMEM((ITERS, LANES), f32),
        ),
        in_specs=[pl.BlockSpec(memory_space=pltpu.HBM)] * 8,
        out_specs=(pl.BlockSpec(memory_space=pltpu.VMEM),) * 3,
        scratch_shapes=[
            pltpu.VMEM((STEPS + 1, 2, 3, wide, full), f32),
            pltpu.VMEM((STEPS, 2, 4, wide, full), f32),
            pltpu.VMEM((STEPS, 2, 3, wide, full), f32),
            pltpu.VMEM((2, 3, rows, full), f32),
            pltpu.VMEM((3, rows, lon), f32),
            pltpu.VMEM((2, cols, n_obs), jnp.bfloat16),
            pltpu.VMEM((2, 8, n_obs), f32),
            pltpu.VMEM((wide, full), f32),
            pltpu.VMEM((wide, LANES), f32),
            pltpu.VMEM((wide, LANES), f32),
            pltpu.VMEM(field, f32),
            pltpu.VMEM(field, f32),
            pltpu.VMEM(field, f32),
            pltpu.VMEM((ITERS,) + field, f32),
            pltpu.VMEM((ITERS, 2, 3, rows, full), f32),
            pltpu.VMEM((ITERS,) + edge, f32),
            pltpu.VMEM((ITERS, 2, 3, wide, full), f32),
            pltpu.VMEM((ITERS,) + edge, f32),
            pltpu.VMEM((ITERS,) + field, f32),
            pltpu.VMEM((ITERS, n_tm * n_lat if direct else n_lat, 2, LANES), f32),
            pltpu.VMEM((ITERS, n_tm, 2, LANES), f32),
            pltpu.VMEM(field, f32),
            pltpu.VMEM((ITERS,) + field, f32),
            pltpu.VMEM(field, f32),
            pltpu.VMEM(args[3].shape, jnp.int32),
            pltpu.VMEM((1, n_obs), jnp.int32),
            pltpu.VMEM((1, n_obs), jnp.int32),
            pltpu.VMEM((1, n_obs), f32),
            pltpu.VMEM((1, n_obs), f32),
            pltpu.SemaphoreType.DMA((sems,)),
            pltpu.SemaphoreType.DMA((sems,)),
            pltpu.SemaphoreType.DMA((7 + ITERS,)),
            pltpu.SemaphoreType.REGULAR((max(n_tm.bit_length(), 1),)),
        ],
        compiler_params=pltpu.CompilerParams(
            collective_id=0, has_side_effects=True, vmem_limit_bytes=KERNEL_VMEM
        ),
    )(*[pltpu.with_memory_space_constraint(a, pltpu.HBM) for a in args])
    return pl.pallas_call(
        write_out,
        out_shape=(
            jax.ShapeDtypeStruct(states.shape, f32),
            jax.ShapeDtypeStruct(states.shape, f32),
            jax.ShapeDtypeStruct((ITERS,), f32),
        ),
        in_specs=[pl.BlockSpec(memory_space=pltpu.VMEM)] * 3,
        out_specs=(pl.BlockSpec(memory_space=pltpu.HBM),) * 3,
        scratch_shapes=[pltpu.SMEM((ITERS,), f32), pltpu.SemaphoreType.DMA((3,))],
        compiler_params=pltpu.CompilerParams(vmem_limit_bytes=WRITE_VMEM),
    )(est, slid, costs)


def solution(mesh):
    placed = (
        P("tm", None, "lat", None),
        P(None, "lat", None),
        P(None, "lat", None),
        P("lat", None),
        P("tm", "lat"),
        P("tm", "lat"),
        P("tm", "lat"),
        P("tm", "lat"),
    )
    return jax.shard_map(
        functools.partial(shards, mesh.shape["tm"], mesh.shape["lat"]),
        mesh=mesh,
        in_specs=placed,
        out_specs=(P("tm", None, "lat", None), P("tm", None, "lat", None), P()),
        check_vma=False,
    )
```

```python
import functools

import jax
import jax.numpy as jnp
from jax import lax
from jax.experimental import pallas as pl
from jax.experimental.pallas import tpu as pltpu
from jax.sharding import PartitionSpec as P

STEPS = 4
ITERS = 2
TILE_LAT = 4
TILE_LON = 16

TIME_STEP = 0.25
MEAN_DEPTH = 1.0
DRAG_RATE = 0.02
STEP_LENGTH = 0.3
CORIOLIS_MEAN = 0.3
CORIOLIS_SLOPE = 0.2
EPSILON = 1e-06

MESH = pl.DeviceIdType.MESH
LANES = 128
DIRECT_MAX = 64
KERNEL_VMEM = 24 * 2**20
WRITE_VMEM = 2**20


def split3(x):
    hi = x.astype(jnp.bfloat16)
    rest = x - hi.astype(jnp.float32)
    mid = rest.astype(jnp.bfloat16)
    low = (rest - mid.astype(jnp.float32)).astype(jnp.bfloat16)
    return jnp.concatenate([hi, mid, low], axis=0)


def join3(y):
    n = y.shape[0] // 3
    return (y[2 * n :] + y[n : 2 * n]) + y[:n]


def fold_lanes(x):
    total = x[:, :LANES]
    for c in range(LANES, x.shape[1], LANES):
        total = total + x[:, c : c + LANES]
    return jnp.sum(total, axis=0, keepdims=True)


def kernel(
    n_tm, n_lat,
    states_hbm, background_hbm, error_hbm, mask_hbm, cells_hbm, moments_hbm, values_hbm, obs_err_hbm,
    est_out, slid_out, costs_out,
    xs, deriv, lam, pack, whole, onehot, obs, gain, cor, masks, variance, inv_var,
    xnext, fe_prev, adj_in, adj_col, dirs, dir_edge, dir_next, parts, parts_tm,
    slid_base, est_dir, slid_dir,
    land_mask, obs_cells, obs_moments, obs_values, obs_error,
    ssem, rsem, lsem, known,
):
    tm = lax.axis_index("tm")
    lat = lax.axis_index("lat")
    rows, cols = variance.shape[1], variance.shape[2]
    lon = whole.shape[2]
    full = gain.shape[1]
    wide = 2 * rows
    half = STEPS
    total_rows = rows * n_lat
    cell_count = 3 * total_rows * lon
    n_dev = n_tm * n_lat
    n_pair = n_tm // 2
    me = tm * n_lat + lat
    side = lax.rem(tm, 2)
    mate = 1 - side
    pair = lax.div(tm, 2)
    even = side == 0
    odd = side == 1
    has_up = lat > 0
    has_down = lat < n_lat - 1
    has_prev = pair > 0
    has_next = pair < n_pair - 1
    is_last = pair == n_pair - 1
    core = lax.rem(lat, 2)
    up_far, down_near = has_up & (core == 0), has_down & (core == 0)
    up_near, down_far = has_up & (core == 1), has_down & (core == 1)
    across_tm = tm + 1 - 2 * side
    up = {"lat": lat - 1}
    down = {"lat": lat + 1}
    across = {"tm": across_tm}
    across_up = {"tm": across_tm, "lat": lat - 1}
    across_down = {"tm": across_tm, "lat": lat + 1}
    before = {"tm": tm - 2}
    after = {"tm": tm + 2}
    left = {"tm": tm - 1}
    right = {"tm": tm + 1}
    direct = n_dev <= DIRECT_MAX

    def wrapped(i, n):
        return jnp.where(i >= n, i - n, i)

    lats = [lat] + [wrapped(lat + d, n_lat) for d in range(1, n_lat)]
    tms = [tm] + [wrapped(tm + d, n_tm) for d in range(1, n_tm)]
    lat_partners = [{"lat": lats[d]} for d in range(1, n_lat)]
    tm_partners = [{"tm": tms[d]} for d in range(1, n_tm)]
    if direct:
        pairs = [(t, d) for t in range(n_tm) for d in range(n_lat) if t or d]
        if n_tm & (n_tm - 1) == 0 and n_lat & (n_lat - 1) == 0:
            pairs.sort(key=lambda p: -(p[0] // 2 + p[0] % 2 + p[1] // 2 + 0.1 * (p[1] % 2)))
            all_partners = [
                {"tm": jnp.bitwise_xor(tm, t), "lat": jnp.bitwise_xor(lat, d)} for t, d in pairs
            ]
        else:
            all_partners = [{"tm": tms[t], "lat": lats[d]} for t, d in pairs]

    def guarded(cond, action):
        if cond is None:
            action()
        else:
            pl.when(cond)(action)

    barrier = pltpu.get_barrier_semaphore()
    greeted = [(None, p) for p in lat_partners]
    greeted += [(None, {"tm": across_tm, "lat": lats[d]}) for d in range(n_lat)]
    greeted += [
        (has_prev, before), (has_next, after), (even & has_prev, left), (odd & has_next, right),
    ]
    for cond, partner in greeted:
        guarded(cond, lambda partner=partner: pl.semaphore_signal(
            barrier, inc=1, device_id=partner, device_id_type=MESH))
    reaches = []
    while 2 ** len(reaches) < n_pair:
        reaches.append(2 ** len(reaches))

    def tell(stage):
        d = reaches[stage]
        for cond, target in ((pair >= d, tm - 2 * d), (pair + d < n_pair, tm + 2 * d)):
            @pl.when(cond)
            def _(target=target):
                pl.semaphore_signal(
                    known.at[stage], inc=1, device_id={"tm": target}, device_id_type=MESH
                )

    def hear(stage):
        d = reaches[stage]
        pl.semaphore_wait(
            known.at[stage],
            (pair >= d).astype(jnp.int32) + (pair + d < n_pair).astype(jnp.int32),
        )

    own = slice(0, rows)
    mine = slice(0, cols)
    edge = slice(cols, full)
    loads = []
    my_cols = pl.ds(pl.multiple_of(side * cols, LANES), cols)

    def load(src, dst):
        copy = pltpu.make_async_copy(src, dst, lsem.at[len(loads)])
        copy.start()
        loads.append(copy)

    load(states_hbm.at[0], whole)
    load(mask_hbm, land_mask)
    load(cells_hbm, obs_cells)
    load(moments_hbm, obs_moments)
    load(values_hbm, obs_values)
    load(obs_err_hbm, obs_error)
    load(error_hbm.at[:, :, my_cols], variance)
    for it in range(ITERS):
        @pl.when(pair == 0)
        def _(it=it):
            pltpu.make_async_copy(
                background_hbm.at[:, :, my_cols], fe_prev.at[it], lsem.at[7 + it]
            ).start()

    def remote(src, dst, k, device):
        return pltpu.make_async_remote_copy(
            src_ref=src, dst_ref=dst, send_sem=ssem.at[k], recv_sem=rsem.at[k],
            device_id=device, device_id_type=MESH,
        )

    pending = []
    late = []

    def send(cond, src, dst, k, device, queue=pending):
        guarded(cond, lambda: remote(src, dst, k, device).start())
        queue.append((cond, src, k, device))

    def drain(queue):
        for cond, src, k, device in queue:
            guarded(cond, lambda src=src, k=k, device=device: remote(src, src, k, device).wait_send())
        queue.clear()

    def arrive(cond, dst, k, device):
        guarded(cond, lambda: remote(dst, dst, k, device).wait_recv())

    lo, hi = slice(0, half), slice(half, rows)
    lo_w, hi_w = slice(rows, rows + half), slice(rows + half, wide)

    @pl.when(lat == n_lat - 1)
    def _():
        xs[0, :, :, lo_w] = jnp.zeros((2, 3, half, full), jnp.float32)
        masks[lo_w, :] = jnp.zeros((half, LANES), jnp.float32)
        for it in range(ITERS):
            adj_in[it, :, :, hi] = jnp.zeros((2, 3, half, full), jnp.float32)
            dirs[it, :, :, lo_w] = jnp.zeros((2, 3, half, full), jnp.float32)

    @pl.when(lat == 0)
    def _():
        xs[0, :, :, hi_w] = jnp.zeros((2, 3, half, full), jnp.float32)
        masks[hi_w, :] = jnp.zeros((half, LANES), jnp.float32)
        for it in range(ITERS):
            adj_in[it, :, :, lo] = jnp.zeros((2, 3, half, full), jnp.float32)
            dirs[it, :, :, hi_w] = jnp.zeros((2, 3, half, full), jnp.float32)

    @pl.when(is_last)
    def _():
        xnext[...] = jnp.zeros(xnext.shape, jnp.float32)
        for it in range(ITERS):
            dir_next[it] = jnp.zeros(xnext.shape, jnp.float32)

    loads[1].wait()
    mask = land_mask[...].astype(jnp.float32)
    tile_cols = mask.shape[1]
    masks[own, :] = jnp.concatenate(
        [jnp.broadcast_to(mask[i : i + 1], (TILE_LAT, tile_cols)) for i in range(rows // TILE_LAT)],
        axis=0,
    )

    lane = lax.broadcasted_iota(jnp.int32, (rows, LANES), 1)
    first_lanes = lane < half
    last_lanes = lane >= LANES - half

    def border(first, last):
        return jnp.where(first_lanes, first, jnp.where(last_lanes, last, 0.0))

    loads[0].wait()
    for h in range(2):
        for f in range(3):
            c, o = h * cols, (1 - h) * cols
            pack[h, f, :, mine] = whole[f, :, c : c + cols]
            pack[h, f, :, edge] = border(
                whole[f, :, o : o + LANES], whole[f, :, o + cols - LANES : o + cols]
            )
    for copy in loads[2:6]:
        copy.wait()
    n_obs = obs_cells.shape[1]
    obs[side] = jnp.concatenate(
        [
            obs_cells[...].astype(jnp.float32), obs_moments[...].astype(jnp.float32),
            obs_values[...], obs_error[...], jnp.zeros((4, n_obs), jnp.float32),
        ],
        axis=0,
    )
    pl.semaphore_wait(
        barrier,
        2 * n_lat - 1 + has_prev.astype(jnp.int32) + has_next.astype(jnp.int32)
        + (even & has_prev).astype(jnp.int32) + (odd & has_next).astype(jnp.int32),
    )

    send(has_up, masks.at[lo], masks.at[lo_w], 0, up)
    send(has_down, masks.at[hi], masks.at[hi_w], 1, down)
    send(None, obs.at[side], obs.at[side], 7, across)
    send(has_up, pack.at[side, :, lo], xs.at[0, side, :, lo_w], 5, up)
    send(has_down, pack.at[side, :, hi], xs.at[0, side, :, hi_w], 6, down)
    send(None, pack.at[mate], xs.at[0, side, :, own], 2, across)
    send(up_far, pack.at[mate, :, lo], xs.at[0, side, :, lo_w], 3, across_up)
    send(down_far, pack.at[mate, :, hi], xs.at[0, side, :, hi_w], 4, across_down)
    send(even & has_prev, pack.at[0, :, :, mine], xnext, 8, before)
    send(even & has_prev, pack.at[1, :, :, mine], xnext, 9, left)
    if reaches:
        tell(0)

    xs[0, side, :, own] = pack[side]
    loads[6].wait()
    var = variance[...] * variance[...]
    variance[...] = var
    inv_var[...] = 1.0 / var
    r_id = lax.broadcasted_iota(jnp.int32, (wide, LANES), 0)
    r_id = jnp.where(r_id < rows + half, r_id, r_id - wide) + lat * rows
    cor[...] = 2.0 * (CORIOLIS_MEAN + CORIOLIS_SLOPE * (r_id.astype(jnp.float32) / total_rows - 0.5))
    first_col = lax.broadcasted_iota(jnp.int32, (tile_cols, full), 0) * TILE_LON
    place = lax.broadcasted_iota(jnp.int32, (tile_cols, full), 1)
    col = jnp.where(place < cols + half, place, place - full) + side * cols
    col = jnp.where(col >= lon, col - lon, jnp.where(col < 0, col + lon, col))
    used = (place < cols + half) | (place >= full - half)
    grow = (used & (col >= first_col) & (col < first_col + TILE_LON)).astype(jnp.float32).astype(jnp.bfloat16)

    arrive(None, obs.at[mate], 7, across)
    valid, taken, targets, precision = [], [], [], []
    for w in range(2):
        cells = obs[w, 0:1].astype(jnp.int32)
        cell_row = jnp.zeros_like(cells)
        for r in range(1, rows):
            cell_row = cell_row + (cells >= r * lon).astype(jnp.int32)
        cell_col = cells - cell_row * lon - side * cols
        inside = (cell_col >= 0) & (cell_col < cols)
        onehot[w] = (
            lax.broadcasted_iota(jnp.int32, (cols, n_obs), 0) == cell_col
        ).astype(jnp.float32).astype(jnp.bfloat16)
        valid.append(inside.astype(jnp.float32))
        taken.append((
            (lax.broadcasted_iota(jnp.int32, (STEPS * rows, n_obs), 0)
             == obs[w, 1:2].astype(jnp.int32) * rows + cell_row) & inside
        ).astype(jnp.float32))
        targets.append(obs[w, 2:3])
        precision.append(1.0 / (obs[w, 3:4] * obs[w, 3:4]))

    arrive(has_down, masks.at[lo_w], 0, down)
    arrive(has_up, masks.at[hi_w], 1, up)
    gain[...] = (0.5 * TIME_STEP) * jnp.dot(
        masks[...].astype(jnp.bfloat16), grow, preferred_element_type=jnp.float32,
    )
    arrive(has_down, xs.at[0, side, :, lo_w], 5, down)
    arrive(has_up, xs.at[0, side, :, hi_w], 6, up)

    def east(a):
        return pltpu.roll(a, full - 1, 1)

    def west(a):
        return pltpu.roll(a, 1, 1)

    def north(a):
        return pltpu.roll(a, wide - 1, 0)

    def south(a):
        return pltpu.roll(a, 1, 0)

    def dx2(a):
        return east(a) - west(a)

    def dy2(a):
        return north(a) - south(a)

    def coriolis2(n):
        return jnp.concatenate([cor[0:n]] * (full // LANES), axis=-1)

    def forward_step(s, w, n):
        h, u, v = xs[s, w, 0] + MEAN_DEPTH, xs[s, w, 1], xs[s, w, 2]
        h_n, h_s, u_n, u_s = north(h)[:n], south(h)[:n], north(u)[:n], south(u)[:n]
        v_n, v_s = north(v)[:n], south(v)[:n]
        h, u, v = h[:n], u[:n], v[:n]
        h_e, h_w, u_e, u_w, v_e, v_w = east(h), west(h), east(u), west(u), east(v), west(v)
        g = gain[0:n]
        f2 = coriolis2(n)
        drag_u = (u_e - u_w) + 2.0 * DRAG_RATE
        turn_u = f2 - (u_n - u_s)
        turn_v = f2 + (v_e - v_w)
        drag_v = (v_n - v_s) + 2.0 * DRAG_RATE
        xs[s + 1, w, 0, 0:n] = xs[s, w, 0, 0:n] - g * ((h_e * u_e - h_w * u_w) + (h_n * v_n - h_s * v_s))
        xs[s + 1, w, 1, 0:n] = u + g * (v * turn_u - u * drag_u - (h_e - h_w))
        xs[s + 1, w, 2, 0:n] = v - g * (u * turn_v + v * drag_v + (h_n - h_s))
        return drag_u, turn_u, turn_v, drag_v

    def forward(windows, keep):
        for s in range(STEPS):
            n = rows if s == STEPS - 1 else wide
            for w in windows:
                terms = forward_step(s, w, n)
                if keep:
                    for i, term in enumerate(terms):
                        deriv[s, w, i, 0:n] = term

    def padded(a):
        return jnp.concatenate([a, jnp.zeros((rows, full), jnp.float32)], axis=0)

    def edged(a):
        return jnp.concatenate([a, jnp.zeros((a.shape[0], LANES), jnp.float32)], axis=1)

    def adjoint_last(w, closing, forcing):
        s = STEPS - 1
        g = gain[own]
        top = [edged(c) for c in closing]
        a, b, c = top[0] * g, top[1] * g, top[2] * g
        h, u, v = xs[s, w, 0] + MEAN_DEPTH, xs[s, w, 1, own], xs[s, w, 2]
        b_all, c_all = padded(b), padded(c)
        ax, ay, cy = dx2(a), dy2(padded(a)), dy2(c_all)
        vb, vc = dy2(v * b_all), dy2(v * c_all)
        v_ay, h_ay = v * ay, h * ay
        lam[s, w, 0, own] = top[0] + edged(forcing) + u * ax + v_ay[:rows] + dx2(b) + cy[:rows]
        lam[s, w, 0, rows:wide] = v_ay[rows:] + cy[rows:]
        lam[s, w, 1, own] = (
            top[1] + h[:rows] * ax + dx2(u * b) + vb[:rows]
            - b * deriv[s, w, 0, own] - c * deriv[s, w, 2, own]
        )
        lam[s, w, 1, rows:wide] = vb[rows:]
        lam[s, w, 2, own] = (
            top[2] + h_ay[:rows] + dx2(u * c) + vc[:rows]
            + b * deriv[s, w, 1, own] - c * deriv[s, w, 3, own]
        )
        lam[s, w, 2, rows:wide] = h_ay[rows:] + vc[rows:]

    def adjoint_step(s, w, forcing):
        g = gain[...]
        lh, lu, lv = lam[s + 1, w, 0], lam[s + 1, w, 1], lam[s + 1, w, 2]
        a, b, c = lh * g, lu * g, lv * g
        h, u, v = xs[s, w, 0] + MEAN_DEPTH, xs[s, w, 1], xs[s, w, 2]
        ax, ay = dx2(a), dy2(a)
        b_e, b_w, u_e, u_w = east(b), west(b), east(u), west(u)
        c_n, c_s, v_n, v_s = north(c), south(c), north(v), south(v)
        new_h = lh + u * ax + v * ay + (b_e - b_w) + (c_n - c_s)
        lam[s, w, 0, own] = new_h[:rows] + edged(forcing)
        lam[s, w, 0, rows:wide] = new_h[rows:]
        lam[s, w, 1] = (
            lu + h * ax + (u_e * b_e - u_w * b_w) + dy2(v * b)
            - b * deriv[s, w, 0] - c * deriv[s, w, 2]
        )
        lam[s, w, 2] = (
            lv + h * ay + dx2(u * c) + (v_n * c_n - v_s * c_s)
            + b * deriv[s, w, 1] - c * deriv[s, w, 3]
        )

    def exchange(buf, value, k, mine_at, partner):
        buf[mine_at] = value
        for device in partner:
            remote(buf.at[mine_at], buf.at[mine_at], k, device).start()

    def collect(buf, k, size, partner):
        remote(buf.at[0 : size - 1], buf.at[0 : size - 1], k, partner[0]).wait_recv()
        return jnp.sum(buf[...], axis=0)

    def sent(buf, k, size, partner):
        remote(buf.at[0 : size - 1], buf.at[0 : size - 1], k, partner[0]).wait_send()

    scale = None
    scales = []
    est_k = [28 + 14 * ITERS + it for it in range(ITERS)]
    for it in range(ITERS):
        base = 10 + 13 * it
        last = it == ITERS - 1
        if it == 0:
            forward((side,), True)
            arrive(None, xs.at[0, mate, :, own], 2, across)
            k_near = 28 + 15 * ITERS
            send(up_near, xs.at[0, mate, :, lo], xs.at[0, mate, :, lo_w], k_near, up)
            send(down_near, xs.at[0, mate, :, hi], xs.at[0, mate, :, hi_w], k_near + 1, down)
            arrive(down_far, xs.at[0, mate, :, lo_w], 3, across_down)
            arrive(up_far, xs.at[0, mate, :, hi_w], 4, across_up)
            arrive(down_near, xs.at[0, mate, :, lo_w], k_near, down)
            arrive(up_near, xs.at[0, mate, :, hi_w], k_near + 1, up)
            if len(reaches) > 1:
                hear(0)
                tell(1)
            forward((mate,), True)
        else:
            forward((1,), True)
        send(has_next, xs.at[STEPS, 1, :, own, mine], fe_prev.at[it], base, after)
        if it > 0:
            forward((0,), True)

        misfits, weights, spreads = [], [], []
        for w in range(2):
            heights = jnp.concatenate([xs[s, w, 0, own, mine] for s in range(STEPS)], axis=0)
            seen = join3(
                jnp.dot(split3(heights), onehot[w], preferred_element_type=jnp.float32)
            )
            misfit = jnp.sum(seen * taken[w], axis=0, keepdims=True) - targets[w] * valid[w]
            weighted = misfit * precision[w]
            spreads.append(join3(
                lax.dot_general(
                    split3(taken[w] * weighted), onehot[w], (((1,), (1,)), ((), ())),
                    preferred_element_type=jnp.float32,
                )
            ))
            misfits.append(misfit)
            weights.append(weighted)

        def forcing(s, w):
            return spreads[w][s * rows : (s + 1) * rows]

        def state(s, w, f):
            return xs[s, w, f, own, mine]

        for w in range(2):
            if w == 0:
                closing = [(state(STEPS, 0, f) - state(0, 1, f)) * inv_var[f] for f in range(3)]
            else:
                if it == 0:
                    arrive(even & has_next, xnext, 8, after)
                    arrive(odd & has_next, xnext, 9, right)
                    for stage in range(1, len(reaches)):
                        hear(stage)
                        if stage + 1 < len(reaches):
                            tell(stage + 1)
                    if len(reaches) == 1:
                        hear(0)
                else:
                    arrive(has_next, dir_next.at[it - 1], base - 13 + 11, after)
                    xnext[...] = xnext[...] - scale * dir_next[it - 1]
                closing = [
                    jnp.where(has_next, (state(STEPS, 1, f) - xnext[f]) * inv_var[f], 0.0)
                    for f in range(3)
                ]
            adjoint_last(w, closing, forcing(STEPS - 1, w))
            for s in reversed(range(STEPS - 1)):
                adjoint_step(s, w, forcing(s, w))
            k = base + 1 if w == 0 else 30 + 15 * ITERS + 5 * it
            send(None, lam.at[0, w, :, own, edge], adj_col.at[it, w], k + 2, across)
            send(has_down, lam.at[0, w, :, lo_w, edge], adj_in.at[it, w, :, lo, edge], k + 3, across_down)
            send(has_up, lam.at[0, w, :, hi_w, edge], adj_in.at[it, w, :, hi, edge], k + 4, across_up)
            send(has_down, lam.at[0, w, :, lo_w, mine], adj_in.at[it, w, :, lo, mine], k, down)
            send(has_up, lam.at[0, w, :, hi_w, mine], adj_in.at[it, w, :, hi, mine], k + 1, up)
        if last:
            send(odd, xs.at[0, 1, :, own, mine], slid_base, base + 14, across)
            send(even & has_next, xnext, slid_base, base + 14, across)
        arrive(has_prev, fe_prev.at[it], base, before)

        @pl.when(pair == 0)
        def _():
            pltpu.make_async_copy(
                background_hbm.at[:, :, my_cols], fe_prev.at[it], lsem.at[7 + it]
            ).wait()

        cost = misfits[0] * weights[0] + misfits[1] * weights[1]
        for w in range(2):
            for f in range(3):
                start = fe_prev[it, f] if w == 0 else state(STEPS, 0, f)
                gap = state(0, w, f) - start
                cost = cost + fold_lanes(gap * gap * inv_var[f])
                dirs[it, w, f, own, mine] = gap + variance[f] * lam[0, w, f, own, mine]
        steep = jnp.zeros((1, LANES), jnp.float32)
        zeros_mid = jnp.zeros((rows, cols - 2 * LANES), jnp.float32)
        for w in range(2):
            k = base + 1 if w == 0 else 30 + 15 * ITERS + 5 * it
            arrive(has_up, adj_in.at[it, w, :, lo, mine], k, up)
            arrive(has_down, adj_in.at[it, w, :, hi, mine], k + 1, down)
            arrive(None, adj_col.at[it, w], k + 2, across)
            arrive(has_up, adj_in.at[it, w, :, lo, edge], k + 3, across_up)
            arrive(has_down, adj_in.at[it, w, :, hi, edge], k + 4, across_down)
            for f in range(3):
                sides = adj_in[it, w, f, :, edge] + adj_col[it, w, f]
                extra = jnp.concatenate(
                    [
                        jnp.where(first_lanes, sides, 0.0), zeros_mid,
                        jnp.where(last_lanes, sides, 0.0),
                    ],
                    axis=1,
                )
                direction = dirs[it, w, f, own, mine] + variance[f] * (
                    adj_in[it, w, f, :, mine] + extra
                )
                dirs[it, w, f, own, mine] = direction
                steep = steep + fold_lanes(direction * direction * inv_var[f])
                dir_edge[it, w, f] = border(direction[:, :LANES], direction[:, cols - LANES :])

        message = jnp.concatenate([steep, cost], axis=0)
        if last:
            send(None, dirs.at[it, mate, 0:2, own, mine], est_dir.at[it, 0:2], est_k[it], across, late)
        if direct:
            exchange(parts.at[it], message, base + 12, me, all_partners)
        else:
            exchange(parts.at[it], message, base + 12, lat, lat_partners)
        go_up, go_down, go = (has_up & is_last, has_down & is_last, is_last) if last else (has_up, has_down, None)
        send(go_up, dirs.at[it, :, :, lo, mine], dirs.at[it, :, :, lo_w, mine], base + 6, up, late)
        send(go_down, dirs.at[it, :, :, hi, mine], dirs.at[it, :, :, hi_w, mine], base + 7, down, late)
        send(go, dir_edge.at[it], dirs.at[it, :, :, own, edge], base + 8, across, late)
        send(go_up, dir_edge.at[it, :, :, lo], dirs.at[it, :, :, lo_w, edge], base + 9, across_up, late)
        send(go_down, dir_edge.at[it, :, :, hi], dirs.at[it, :, :, hi_w, edge], base + 10, across_down, late)

        def send_on():
            if last:
                send(None, dirs.at[it, mate, 2:3, own, mine], est_dir.at[it, 2:3], base + 13, across, late)
                send(odd, dirs.at[it, 1, :, own, mine], slid_dir, base + 16, across, late)
                send(even & has_prev, dirs.at[it, 0, :, own, mine], slid_dir, base + 17, left, late)
                send(odd & has_prev, dirs.at[it, 0, :, own, mine], dir_next.at[it], base + 11, before, late)
            else:
                send(has_prev, dirs.at[it, 0, :, own, mine], dir_next.at[it], base + 11, before, late)
                send(None, dirs.at[it, mate, :, own, mine], est_dir.at[it], est_k[it], across, late)
            drain(pending)

        if direct:
            send_on()
            total = collect(parts.at[it], base + 12, n_dev, all_partners)
        else:
            total = collect(parts.at[it], base + 12, n_lat, lat_partners)
            k_tm = 28 + 13 * ITERS + it
            exchange(parts_tm.at[it], total, k_tm, tm, tm_partners)
            send_on()
            total = collect(parts_tm.at[it], k_tm, n_tm, tm_partners)
        steepness = jnp.sum(total[0:1], axis=1, keepdims=True)
        scale = STEP_LENGTH / jnp.sqrt(steepness / (n_tm * cell_count) + EPSILON)
        scales.append(scale)
        costs_out[it : it + 1] = jnp.broadcast_to(
            jnp.sum(total[1:2], axis=1, keepdims=True) * (0.5 / cell_count), (1, LANES)
        )

        for w in range(2):
            for f in range(3):
                xs[0, w, f, own, mine] = state(0, w, f) - scale * dirs[it, w, f, own, mine]
        arrive(go if not last else is_last, dirs.at[it, :, :, own, edge], base + 8, across)
        arrive(go_down, dirs.at[it, :, :, lo_w, mine], base + 6, down)
        arrive(go_up, dirs.at[it, :, :, hi_w, mine], base + 7, up)
        arrive(go_down, dirs.at[it, :, :, lo_w, edge], base + 9, across_down)
        arrive(go_up, dirs.at[it, :, :, hi_w, edge], base + 10, across_up)

        def halos(it=it, windows=(1,) if last else (0, 1), scale=scale):
            for w in windows:
                for f in range(3):
                    xs[0, w, f, own, edge] = xs[0, w, f, own, edge] - scale * dirs[it, w, f, own, edge]
                    xs[0, w, f, rows:wide] = xs[0, w, f, rows:wide] - scale * dirs[it, w, f, rows:wide]

        guarded(is_last if last else None, halos)

    end = 10 + 13 * (ITERS - 1)
    k_end = end + 18

    @pl.when(is_last)
    def _():
        forward((1,), False)

    send(even & is_last, xs.at[STEPS, 1, :, own, mine], slid_dir, k_end, across, late)

    for h in range(2):
        c, o = slice(h * cols, (h + 1) * cols), slice((1 - h) * cols, (2 - h) * cols)

        @pl.when(side == h)
        def _(h=h, c=c):
            est_out[0, :, :, c] = xs[0, h, :, own, mine]
            if h == 0:
                slid_out[0, :, :, c] = xs[0, 1, :, own, mine]

    drain(late)
    for it in range(ITERS):
        base = 10 + 13 * it
        if direct:
            sent(parts.at[it], base + 12, n_dev, all_partners)
        else:
            sent(parts.at[it], base + 12, n_lat, lat_partners)
            sent(parts_tm.at[it], 28 + 13 * ITERS + it, n_tm, tm_partners)

    arrive(even, slid_base, end + 14, across)
    arrive(odd & has_next, slid_base, end + 14, across)
    for it in range(ITERS - 1):
        arrive(None, est_dir.at[it], est_k[it], across)
    arrive(None, est_dir.at[ITERS - 1, 0:2], est_k[ITERS - 1], across)
    arrive(None, est_dir.at[ITERS - 1, 2:3], end + 13, across)
    moved = [scales[it] * est_dir[it] for it in range(ITERS)]
    for h in range(2):
        o = slice((1 - h) * cols, (2 - h) * cols)

        @pl.when(side == h)
        def _(o=o):
            other = whole[:, :, o]
            for it in range(ITERS):
                other = other - moved[it]
            est_out[0, :, :, o] = other

    arrive(even, slid_dir, end + 16, across)
    arrive(odd & has_next, slid_dir, end + 17, right)
    arrive(odd & has_next, dir_next.at[ITERS - 1], end + 11, after)
    arrive(odd & is_last, slid_dir, k_end, across)

    @pl.when(even)
    def _():
        slid_out[0, :, :, cols:] = slid_base[...] - scale * slid_dir[...]

    @pl.when(odd & has_next)
    def _():
        slid_out[0, :, :, 0:cols] = slid_base[...] - scale * slid_dir[...]
        slid_out[0, :, :, cols:] = xnext[...] - scale * dir_next[ITERS - 1]

    @pl.when(odd & is_last)
    def _():
        slid_out[0, :, :, 0:cols] = slid_dir[...]
        slid_out[0, :, :, cols:] = xs[STEPS, 1, :, own, mine]


def write_out(est, slid, costs, est_out, slid_out, costs_out, held, sem):
    moves = [
        pltpu.make_async_copy(est, est_out, sem.at[0]),
        pltpu.make_async_copy(slid, slid_out, sem.at[1]),
        pltpu.make_async_copy(held, costs_out, sem.at[2]),
    ]
    moves[0].start()
    moves[1].start()
    for it in range(ITERS):
        held[it] = costs[it, 0]
    moves[2].start()
    for copy in moves:
        copy.wait()


def shards(n_tm, n_lat, *args):
    states, background = args[0], args[1]
    _, rows, lon = background.shape
    n_obs = args[4].shape[1]
    wide, cols = 2 * rows, lon // 2
    full = cols + LANES
    f32 = jnp.float32
    direct = n_tm * n_lat <= DIRECT_MAX
    field = (3, rows, cols)
    edge = (2, 3, rows, LANES)
    sems = 30 + 20 * ITERS
    est, slid, costs = pl.pallas_call(
        functools.partial(kernel, n_tm, n_lat),
        out_shape=(
            pltpu.VMEM(states.shape, f32),
            pltpu.VMEM(states.shape, f32),
            pltpu.VMEM((ITERS, LANES), f32),
        ),
        in_specs=[pl.BlockSpec(memory_space=pltpu.HBM)] * 8,
        out_specs=(pl.BlockSpec(memory_space=pltpu.VMEM),) * 3,
        scratch_shapes=[
            pltpu.VMEM((STEPS + 1, 2, 3, wide, full), f32),
            pltpu.VMEM((STEPS, 2, 4, wide, full), f32),
            pltpu.VMEM((STEPS, 2, 3, wide, full), f32),
            pltpu.VMEM((2, 3, rows, full), f32),
            pltpu.VMEM((3, rows, lon), f32),
            pltpu.VMEM((2, cols, n_obs), jnp.bfloat16),
            pltpu.VMEM((2, 8, n_obs), f32),
            pltpu.VMEM((wide, full), f32),
            pltpu.VMEM((wide, LANES), f32),
            pltpu.VMEM((wide, LANES), f32),
            pltpu.VMEM(field, f32),
            pltpu.VMEM(field, f32),
            pltpu.VMEM(field, f32),
            pltpu.VMEM((ITERS,) + field, f32),
            pltpu.VMEM((ITERS, 2, 3, rows, full), f32),
            pltpu.VMEM((ITERS,) + edge, f32),
            pltpu.VMEM((ITERS, 2, 3, wide, full), f32),
            pltpu.VMEM((ITERS,) + edge, f32),
            pltpu.VMEM((ITERS,) + field, f32),
            pltpu.VMEM((ITERS, n_tm * n_lat if direct else n_lat, 2, LANES), f32),
            pltpu.VMEM((ITERS, n_tm, 2, LANES), f32),
            pltpu.VMEM(field, f32),
            pltpu.VMEM((ITERS,) + field, f32),
            pltpu.VMEM(field, f32),
            pltpu.VMEM(args[3].shape, jnp.int32),
            pltpu.VMEM((1, n_obs), jnp.int32),
            pltpu.VMEM((1, n_obs), jnp.int32),
            pltpu.VMEM((1, n_obs), f32),
            pltpu.VMEM((1, n_obs), f32),
            pltpu.SemaphoreType.DMA((sems,)),
            pltpu.SemaphoreType.DMA((sems,)),
            pltpu.SemaphoreType.DMA((7 + ITERS,)),
            pltpu.SemaphoreType.REGULAR((max(n_tm.bit_length(), 1),)),
        ],
        compiler_params=pltpu.CompilerParams(
            collective_id=0, has_side_effects=True, vmem_limit_bytes=KERNEL_VMEM
        ),
    )(*[pltpu.with_memory_space_constraint(a, pltpu.HBM) for a in args])
    return pl.pallas_call(
        write_out,
        out_shape=(
            jax.ShapeDtypeStruct(states.shape, f32),
            jax.ShapeDtypeStruct(states.shape, f32),
            jax.ShapeDtypeStruct((ITERS,), f32),
        ),
        in_specs=[pl.BlockSpec(memory_space=pltpu.VMEM)] * 3,
        out_specs=(pl.BlockSpec(memory_space=pltpu.HBM),) * 3,
        scratch_shapes=[pltpu.SMEM((ITERS,), f32), pltpu.SemaphoreType.DMA((3,))],
        compiler_params=pltpu.CompilerParams(vmem_limit_bytes=WRITE_VMEM),
    )(est, slid, costs)


def solution(mesh):
    placed = (
        P("tm", None, "lat", None),
        P(None, "lat", None),
        P(None, "lat", None),
        P("lat", None),
        P("tm", "lat"),
        P("tm", "lat"),
        P("tm", "lat"),
        P("tm", "lat"),
    )
    return jax.shard_map(
        functools.partial(shards, mesh.shape["tm"], mesh.shape["lat"]),
        mesh=mesh,
        in_specs=placed,
        out_specs=(P("tm", None, "lat", None), P("tm", None, "lat", None), P()),
        check_vma=False,
    )
```
